256 devices in a mesh: lag: 32 (over y, z_lo, x), space: 8 (over z_hi, core).
Axes of the slice: x: 4, y: 4, z: 8 (z_hi: 4, z_lo: 2; z = z_hi * 2 + z_lo), core: 2. Of those that a mesh axis runs over, the one named last changes fastest.
Arguments:
- ensemble: bfloat16 [32, 1024, 1024], P('lag', 'space'), may hold values from -6 to 6
- slot_order: int32 [32], replicated, may hold values from 0 to 31, each once
- neighbour_shift: int32 [6, 1024], P(None, 'space'), may hold values from -16 to 16, as said below
- edge_coupling: float32 [6, 1024], P(None, 'space'), may hold values from 0.02 to 0.15
- observation_cells: int32 [2, 4, 128], P(None, None, 'space'), may hold values from 0 to 127
- observation_weight: float32 [2, 4, 128], P(None, None, 'space'), may hold values from 0.1 to 0.6
- observation_reading: float32 [2, 128], P(None, 'space'), may hold values from -6 to 6
- observation_variance: float32 [2, 128], replicated, may hold values from 0.25 to 2
- observation_jitter: float32 [2, 128, 1024], P(None, 'space'), may hold values from -6 to 6
Outputs:
- analysed: bfloat16 [32, 1024, 1024], P('lag', 'space')
- retired: bfloat16 [2, 1024, 1024], P(None, 'lag', 'space')
The draws below stay inside these ranges and needn't reach their ends.
Inputs may be any that keep to these rules, and one draw needn't show every extreme that they name: `neighbour_shift`: for each cell the 6 offsets are distinct and nonzero. `observation_cells`: observation p reads cells of the partition of 128 cells numbered p // 16.
All inputs are finite; a program needn't handle non-finite values.
Results may differ from the reference program's by a relative error of at most 0.0054.
Values may be sent and summed in bfloat16 or wider, within the bound.
No kernel may reach another device: no remote copies, remote signals or barrier semaphores. Data moves between devices by JAX's collectives and lax.ppermute only.
A program may use at most 64 MiB of HBM per device.

```python
import math
import jax
import jax.numpy as jnp
from jax import lax

MEMBERS = 1024
CELL_DEV = 128
OBS_DEV = 16
NPTS = 4
NBRS = 6
HALO = 16
FC_STEPS = 4
CYCLES = 2
SLABS = 32
NCELLS = 1024
NOBS = 128


def draw_neighbour_shift(key, part):
    scores = jax.random.randint(key, (NCELLS, 2 * HALO), 0, 1 << 20)
    scores = scores * (2 * HALO) + jnp.arange(2 * HALO, dtype=jnp.int32)[None, :]
    unused, picks = lax.top_k(scores, NBRS)
    offsets = jnp.where(picks < HALO, picks - HALO, picks - HALO + 1)
    return offsets.T.astype(jnp.int32)


def place_ends(values, own_key, smallest, largest):
    index_at = [jax.random.randint(jax.random.fold_in(own_key, axis), (), 0, length) for axis, length in enumerate(values.shape)]
    widest = values.shape.index(max(values.shape))
    beside = index_at[:widest] + [(index_at[widest] + 1) % values.shape[widest]] + index_at[widest + 1:]
    return values.at[tuple(index_at)].set(smallest).at[tuple(beside)].set(largest)


def levels(own_key, shape, pieces, smallest, high):
    level = 1.0
    for position, blocks in pieces:
        steps = jax.random.uniform(jax.random.fold_in(jax.random.fold_in(own_key, 6), position), (blocks,), jnp.float32, smallest / len(pieces), high / len(pieces))
        level = level * jnp.repeat(jnp.exp(steps), shape[position] // blocks).reshape((-1,) + (1,) * (len(shape) - 1 - position))
    return level


def noise(rng, dims, scale, limit, split=(), kind=jnp.bfloat16):
    result = scale * jax.random.normal(rng, dims, jnp.float32)
    if split:
        result = result * levels(rng, dims, split, -0.22, 0.18)
    return jnp.clip(result, -limit, limit).astype(kind)


def setup_inputs(seed: int = 0) -> dict:
    keys = jax.random.split(jax.random.key(seed), 10)
    return {
        "ensemble": noise(keys[0], (SLABS, NCELLS, MEMBERS), 1.0, 6.0, ((0, 32), (1, 8))),
        "slot_order": jax.random.permutation(keys[1], SLABS).astype(jnp.int32),
        "neighbour_shift": draw_neighbour_shift(jax.random.fold_in(keys[9], 71), 0),
        "edge_coupling": jnp.clip(jnp.exp(math.log(0.15) - 2.014903 * jax.random.uniform(keys[3], (NBRS, NCELLS), jnp.float32) ** levels(keys[3], (NBRS, NCELLS), ((1, 8),), -0.2, 0.2)), 0.02, 0.15),
        "observation_cells": place_ends(jax.random.randint(keys[4], (CYCLES, NPTS, NOBS), 0, CELL_DEV), jax.random.fold_in(keys[4], 1), 0, CELL_DEV - 1).astype(jnp.int32),
        "observation_weight": jnp.clip(0.1 + 0.5 * jax.random.uniform(keys[5], (CYCLES, NPTS, NOBS), jnp.float32) ** levels(keys[5], (CYCLES, NPTS, NOBS), ((2, 8),), -0.2, 0.2), 0.1, 0.6),
        "observation_reading": noise(keys[6], (CYCLES, NOBS), 1.0, 6.0, ((1, 8),), jnp.float32),
        "observation_variance": jnp.clip(jnp.exp(jax.random.uniform(keys[7], (CYCLES, NOBS), jnp.float32, math.log(0.25), math.log(2.0))), 0.25, 2.0),
        "observation_jitter": noise(keys[8], (CYCLES, NOBS, MEMBERS), 1.0, 6.0, ((1, 8),), jnp.float32),
    }


highest = lax.Precision.HIGHEST

def step_forward(present_state, offsets, coefficients):
    field_f = present_state.astype(jnp.float32)
    anchor = jnp.arange(field_f.shape[0], dtype=jnp.int32) + HALO
    for repeat in range(FC_STEPS):
        padded = jnp.pad(field_f, ((HALO, HALO), (0, 0)))
        accrued = jnp.zeros_like(field_f)
        for neighbour in range(NBRS):
            picked = (anchor + offsets[neighbour]).astype(jnp.int32)
            accrued = accrued + coefficients[neighbour][:, None] * (padded[picked] - field_f)
        field_f = field_f + accrued
    return field_f.astype(jnp.bfloat16)

def compute_gain_weights(predict_ahead, vertex_list, vertex_weights, observation_readings, member_variance, random_jitter):
    to_single_float = predict_ahead.astype(jnp.float32)
    first_cell = jnp.arange(NOBS, dtype=jnp.int32) // OBS_DEV * CELL_DEV
    measured = jnp.zeros((NOBS, MEMBERS), jnp.float32)
    for corner in range(NPTS):
        picked = (first_cell + vertex_list[corner]).astype(jnp.int32)
        measured = measured + vertex_weights[corner][:, None] * to_single_float[picked]
    centre = lax.optimization_barrier(jnp.mean(measured, axis=1, keepdims=True))
    spread = (measured - centre).astype(jnp.bfloat16)
    innovation = (observation_readings[:, None] + jnp.sqrt(member_variance)[:, None] * random_jitter - measured).astype(jnp.bfloat16)
    spread_f = spread.astype(jnp.float32)
    gram_matrix = jnp.dot(spread_f, spread_f.T, precision=highest) + jnp.diag((MEMBERS - 1) * member_variance)
    factor = jnp.linalg.cholesky(gram_matrix)
    solved = jax.scipy.linalg.cho_solve((factor, True), innovation.astype(jnp.float32)).astype(jnp.bfloat16)
    return jnp.dot(spread_f.T, solved.astype(jnp.float32), precision=highest).astype(jnp.bfloat16)

def assimilate_window(present_state, gain_weights):
    values = present_state.astype(jnp.float32)
    centre = lax.optimization_barrier(jnp.mean(values, axis=1, keepdims=True))
    spread = (values - centre).astype(jnp.bfloat16)
    update = jnp.dot(spread.astype(jnp.float32), gain_weights.astype(jnp.float32), precision=highest)
    return (values + update).astype(jnp.bfloat16)

def reference(ensemble, slot_order, neighbour_shift, edge_coupling, observation_cells, observation_weight, observation_reading, observation_variance, observation_jitter):
    departed = []
    for cycle_number in range(CYCLES):
        forcing_term = slot_order[(SLABS - cycle_number) % SLABS]
        target = slot_order[(SLABS - 1 - cycle_number) % SLABS]
        predict_ahead = step_forward(ensemble[forcing_term], neighbour_shift, edge_coupling)
        gain_weights = compute_gain_weights(predict_ahead, observation_cells[cycle_number], observation_weight[cycle_number], observation_reading[cycle_number], observation_variance[cycle_number], observation_jitter[cycle_number])
        refreshed_state = assimilate_window(predict_ahead, gain_weights)
        ensemble = lax.map(lambda present_state: assimilate_window(present_state, gain_weights), ensemble)
        departed.append(ensemble[target].T)
        ensemble = ensemble.at[target].set(refreshed_state)
    return (ensemble, jnp.stack(departed))
```

```python
import jax
import jax.numpy as jnp
from jax import lax
from jax.experimental import pallas as pl
from jax.experimental.pallas import tpu as pltpu
from jax.sharding import Mesh
from jax.sharding import PartitionSpec as P

FC_STEPS = 4
CYCLES = 2
LAG = ("lag_0", "lag_1", "lag_2")
F32 = jnp.float32
BF16 = jnp.bfloat16
LANES = 128
FIRST_ROWS = 48
SECOND_ROWS = 96
THIRD_ROWS = 224


def split3(x):
    hi = x.astype(BF16).astype(F32)
    mid = (x - hi).astype(BF16).astype(F32)
    low = (x - hi - mid).astype(BF16).astype(F32)
    return hi, mid, low


def to_bf16(x):
    return x.astype(BF16)


def prepare_kernel(
    where, slab, shift, coupling, cells, weight, reading, variance, jitter, slab_t, pieces, extra, tmp
):
    values = slab[...].astype(F32)
    mean = jnp.mean(values, axis=1, keepdims=True)
    turned = values.T
    mean_row = jnp.broadcast_to(mean, (LANES, LANES)).T[0:8]
    hi, mid, low = split3(mean_row)
    row8 = lax.broadcasted_iota(jnp.int32, (8, LANES), 0)
    tail = jnp.where(row8 == 0, hi, jnp.where(row8 == 1, mid, jnp.where(row8 == 2, low, 0.0)))
    tail = to_bf16(jnp.concatenate([tail, jnp.zeros((8, LANES), F32)], axis=0))
    turned = to_bf16(turned)
    slab_t[...] = turned
    for r in range(32):
        pieces[r, 0:32, :] = turned[32 * r : 32 * r + 32]
        pieces[r, 32:48, :] = tail

    lag_rank, space_rank = where[0], where[1]
    tmp[...] = jnp.concatenate([jitter[...], jnp.zeros((96, LANES), F32)], axis=0).T
    noise = tmp[pl.ds(pl.multiple_of(32 * (lag_rank % 4), 32), 32), :]
    lane = lax.broadcasted_iota(jnp.int32, (32, LANES), 1)

    def own_lanes(row, take):
        wide = jnp.broadcast_to(row, (8, LANES))
        return pltpu.roll(wide, take, 1)[0:1]

    back = lax.rem(LANES - 16 * space_rank, LANES)
    var0 = own_lanes(variance[0:1, :], back)
    var1 = pltpu.roll(jnp.broadcast_to(own_lanes(variance[1:2, :], back), (8, LANES)), 16, 1)[0:1]
    var = jnp.where(lane[0:1] < 16, var0, jnp.where(lane[0:1] < 32, var1, 0.0))
    read = reading[...]
    error = read + jnp.sqrt(var) * noise
    hi, mid, low = split3(error)
    packed = jnp.where(
        lane < 32,
        hi,
        jnp.where(lane < 64, pltpu.roll(mid, 32, 1), jnp.where(lane < 96, pltpu.roll(low, 64, 1), 0.0)),
    )
    w_hi, w_mid, w_low = split3(weight[...])
    obs = jnp.concatenate([cells[...].astype(F32), w_hi, w_mid, w_low], axis=0)
    obs = pltpu.roll(obs, 96, 1)
    packed = jnp.where(lane < 96, packed, jnp.where(lane < 112, obs, 0.0))
    c_hi, c_mid, c_low = split3(coupling[...])
    extra[...] = to_bf16(jnp.concatenate([shift[...].astype(F32), c_hi, c_mid, c_low, packed], axis=0))


def select_kernel(order, newest, extra, out):
    piece = to_bf16(jnp.concatenate([newest[0, 0:48].astype(F32)[0:40], extra[...].astype(F32)], axis=0))
    for r in range(out.shape[0]):
        out[r] = piece


def observe_kernel(order, where, got, oldest, older, out, state, fields, common, own, sems):
    blocks = got.shape[0]
    lane8 = lax.broadcasted_iota(jnp.int32, (1, LANES), 1)
    lane40 = lax.broadcasted_iota(jnp.int32, (40, LANES), 1)
    lane32 = lax.broadcasted_iota(jnp.int32, (32, LANES), 1)
    error = [jnp.zeros((32, LANES), F32) for _ in range(CYCLES)]
    obs = jnp.zeros((32, LANES), F32)
    targets, weights = [], []
    for b in range(blocks):
        piece = got[b].astype(F32)
        mean = piece[32:33] + piece[33:34] + piece[34:35]
        state[b] = jnp.concatenate([piece[0:32], jnp.broadcast_to(mean, (8, LANES))], axis=0)
        targets.append((lane8 + piece[40:46].astype(jnp.int32)) & (LANES - 1))
        weights.append(piece[46:52] + piece[52:58] + piece[58:64])
        packed = piece[64:96]
        merged = packed + pltpu.roll(packed, 96, 1) + pltpu.roll(packed, 64, 1)
        mine = (lane32 >= 16 * b) & (lane32 < 16 * b + 16)
        for c in range(CYCLES):
            error[c] = jnp.where(mine, pltpu.roll(merged, (16 * b - 16 * c) % LANES, 1), error[c])
        obs = jnp.where(mine, pltpu.roll(packed, (16 * b + 32) % LANES, 1), obs)
    cells = obs[0:8].astype(jnp.int32)
    cell_weight = obs[8:16] + obs[16:24] + obs[24:32]

    def relax(_, carry):
        now = [state[b] for b in range(blocks)]
        zero = jnp.zeros((40, LANES), F32)
        for b in range(blocks):
            centre = now[b]
            before = now[b - 1] if b else zero
            after = now[b + 1] if b + 1 < blocks else zero
            low = jnp.where(lane40 >= 96, before, centre)
            high = jnp.where(lane40 < 32, after, centre)
            accrued = jnp.zeros_like(centre)
            for k in range(6):
                index = jnp.broadcast_to(targets[b][k : k + 1], (40, LANES))
                picked = jnp.where(
                    lane40 < 64,
                    jnp.take_along_axis(low, index, axis=1),
                    jnp.take_along_axis(high, index, axis=1),
                )
                accrued = accrued + weights[b][k : k + 1] * (picked - centre)
            state[b] = centre + accrued
        return carry

    def measure(values, c):
        total = jnp.zeros((40, LANES), F32)
        for q in range(4):
            row = 4 * c + q
            index = jnp.broadcast_to(cells[row : row + 1], (40, LANES))
            picked = jnp.zeros((40, LANES), F32)
            for b in range(blocks):
                mine = (lane40 >= 16 * b) & (lane40 < 16 * b + 16)
                picked = jnp.where(mine, jnp.take_along_axis(values[b], index, axis=1), picked)
            total = total + cell_weight[row : row + 1] * picked
        return total

    lax.fori_loop(0, FC_STEPS, relax, 0)
    forecast = []
    for b in range(blocks):
        value = state[b]
        rounded = to_bf16(value[0:32])
        fields[0, b] = rounded
        value = jnp.concatenate([rounded.astype(F32), value[32:40]], axis=0)
        state[b] = value
        forecast.append(value)
    seen = measure(forecast, 0)
    common[0:32] = to_bf16(seen[0:32] - seen[32:33])
    common[32:64] = to_bf16(error[0] - seen[0:32])
    lax.fori_loop(0, FC_STEPS, relax, 0)
    again = [state[b] for b in range(blocks)]
    for b in range(blocks):
        fields[1, b] = to_bf16(again[b][0:32])
    seen = measure(again, 1)
    common[64:96] = to_bf16(seen[0:32] - seen[32:33])
    common[96:128] = to_bf16(error[1] - seen[0:32])
    common[128:160] = oldest[0, 0:32, :]
    common[160:192] = older[0, 0:32, :]
    space_rank = where[1]
    own[0] = fields[0, space_rank]
    own[1] = fields[1, space_rank]
    lags = out.shape[0]
    second = order[lags - 2]
    copies = []
    for r in range(lags):
        copies.append(pltpu.make_async_copy(common, out.at[r, pl.ds(0, 192), :], sems.at[0, r]))
        pick = jnp.where(second == r, 1, 0)
        copies.append(pltpu.make_async_copy(own.at[pick], out.at[r, pl.ds(192, 32), :], sems.at[1, r]))
    for copy in copies:
        copy.start()
    for copy in copies:
        copy.wait()


def negative_inverse(a):
    size = a.shape[0]
    rows = lax.broadcasted_iota(jnp.int32, (size, size), 0)
    cols = lax.broadcasted_iota(jnp.int32, (size, size), 1)
    lane = lax.broadcasted_iota(jnp.int32, (1, size), 1)
    for k in range(0, size, 4):
        column = [jnp.broadcast_to(a[:, k + i : k + i + 1], (size, size)) for i in range(4)]
        row = [a[k + i : k + i + 1, :] for i in range(4)]
        d = [[column[j][k + i : k + i + 1, :] for j in range(4)] for i in range(4)]
        pd = 1.0 / (d[0][0] * d[1][1] - d[0][1] * d[0][1])
        p00, p01, p11 = d[1][1] * pd, -d[0][1] * pd, d[0][0] * pd
        e00 = p00 * d[0][2] + p01 * d[1][2]
        e01 = p00 * d[0][3] + p01 * d[1][3]
        e10 = p01 * d[0][2] + p11 * d[1][2]
        e11 = p01 * d[0][3] + p11 * d[1][3]
        s00 = d[2][2] - (d[0][2] * e00 + d[1][2] * e10)
        s01 = d[2][3] - (d[0][2] * e01 + d[1][2] * e11)
        s11 = d[3][3] - (d[0][3] * e01 + d[1][3] * e11)
        sd = 1.0 / (s00 * s11 - s01 * s01)
        t00, t01, t11 = s11 * sd, -s01 * sd, s00 * sd
        g00 = e00 * t00 + e01 * t01
        g01 = e00 * t01 + e01 * t11
        g10 = e10 * t00 + e11 * t01
        g11 = e10 * t01 + e11 * t11
        inv = [
            [p00 + g00 * e00 + g01 * e01, p01 + g00 * e10 + g01 * e11, -g00, -g01],
            [p01 + g00 * e10 + g01 * e11, p11 + g10 * e10 + g11 * e11, -g10, -g11],
            [-g00, -g10, t00, t01],
            [-g01, -g11, t01, t11],
        ]
        kept = jnp.where(((rows >= k) & (rows < k + 4)) | ((cols >= k) & (cols < k + 4)), 0.0, a)
        for i in range(4):
            z = inv[i][0] * row[0] + inv[i][1] * row[1] + inv[i][2] * row[2] + inv[i][3] * row[3]
            for j in range(4):
                z = jnp.where(lane == k + j, -inv[i][j], z)
            col = jnp.where((rows >= k) & (rows < k + 4), jnp.where(rows == k + i, -1.0, 0.0), column[i])
            kept = kept - col * z
        a = kept
    return a


def dot(a, b):
    return lax.dot_general(a, b, (((1,), (0,)), ((), ())), preferred_element_type=F32)


def centred(values):
    return to_bf16(values - jnp.mean(values, axis=0, keepdims=True))


def solve(innovation, gram):
    hi, mid, low = split3(-negative_inverse(gram))
    total = dot(innovation, to_bf16(hi)) + (dot(innovation, to_bf16(mid)) + dot(innovation, to_bf16(low)))
    return to_bf16(total)


def update(solved, gain):
    hi = to_bf16(gain)
    low = to_bf16(gain - hi.astype(F32))
    return dot(solved, hi) + dot(solved, low)


def analyse_kernel(order, where, got, slab_t, variance, analysed, retired, keep):
    lags = got.shape[0]
    lag_rank = where[0]
    members = slab_t.shape[0]
    block = members // lags

    def part(i):
        return got[:, 32 * i : 32 * i + 32, :].reshape(members, LANES)

    eye = lax.broadcasted_iota(jnp.int32, (LANES, LANES), 0) == lax.broadcasted_iota(
        jnp.int32, (LANES, LANES), 1
    )
    mine = pl.ds(pl.multiple_of(lag_rank * block, block), block)

    def gram_of(product, c):
        return product + jnp.where(eye, (members - 1) * variance[c : c + 1, :], 0.0)

    took = (lag_rank == order[lags - 1]) | (lag_rank == order[lags - 2])
    own = jnp.where(took, part(6).astype(F32), slab_t[...].astype(F32))
    first = part(4).astype(F32)
    second = part(5).astype(F32)
    spread_t = part(0)
    spread = spread_t.astype(F32).T.astype(BF16)
    ahead = part(2)
    product = dot(spread, jnp.concatenate([spread_t, centred(own), centred(first), centred(second), ahead], axis=1))
    solved = solve(part(1), gram_of(product[:, 0:128], 0))
    keep[...] = first + update(solved, product[:, 256:384])
    retired[0] = to_bf16(keep[mine, :])
    change = update(solved, jnp.concatenate([product[:, 128:256], product[:, 384:640]], axis=1))
    own = to_bf16(own + change[:, 0:128]).astype(F32)
    second = to_bf16(second + change[:, 128:256]).astype(F32)
    spread_t = centred(ahead.astype(F32) + change[:, 256:384])
    innovation = to_bf16(part(3).astype(F32) - change[:, 256:384])
    spread = spread_t.astype(F32).T.astype(BF16)
    product = dot(spread, jnp.concatenate([spread_t, centred(own), centred(second)], axis=1))
    solved = solve(innovation, gram_of(product[:, 0:128], 1))
    change = update(solved, product[:, 128:384])
    keep[...] = second + change[:, 128:256]
    retired[1] = to_bf16(keep[mine, :])
    analysed[0] = to_bf16((own + change[:, 0:128]).T)


def whole(shape):
    return pl.BlockSpec(shape, lambda i, *_: (0,) * len(shape))


def on_device(
    ensemble,
    slot_order,
    neighbour_shift,
    edge_coupling,
    observation_cells,
    observation_weight,
    observation_reading,
    observation_variance,
    observation_jitter,
):
    lags = lax.axis_size(LAG)
    spaces = lax.axis_size("space")
    where = jnp.stack([lax.axis_index(LAG), lax.axis_index("space")]).astype(jnp.int32)
    per = observation_reading.shape[1]
    wide = ((0, 0), (0, LANES - per))
    cells = jnp.pad(observation_cells.reshape(-1, per), wide)
    weight = jnp.pad(observation_weight.reshape(-1, per), wide)
    reading = jnp.pad(observation_reading.reshape(1, -1), ((0, 0), (0, LANES - 2 * per)))
    jitter = observation_jitter.reshape(-1, observation_jitter.shape[2])
    slab = ensemble[0]
    members = slab.shape[1]

    slab_t, pieces, extra = pl.pallas_call(
        prepare_kernel,
        grid_spec=pltpu.PrefetchScalarGridSpec(
            num_scalar_prefetch=1,
            grid=(1,),
            in_specs=[
                whole(slab.shape),
                whole(neighbour_shift.shape),
                whole(edge_coupling.shape),
                whole(cells.shape),
                whole(weight.shape),
                whole(reading.shape),
                whole(observation_variance.shape),
                pl.BlockSpec((2 * per, LANES), lambda i, w: (0, w[0] // 4)),
            ],
            out_specs=[
                whole((members, LANES)),
                whole((lags, FIRST_ROWS, LANES)),
                whole((SECOND_ROWS - 40, LANES)),
            ],
            scratch_shapes=[pltpu.VMEM((LANES, LANES), F32)],
        ),
        out_shape=[
            jax.ShapeDtypeStruct((members, LANES), BF16),
            jax.ShapeDtypeStruct((lags, FIRST_ROWS, LANES), BF16),
            jax.ShapeDtypeStruct((SECOND_ROWS - 40, LANES), BF16),
        ],
        name="prepare",
    )(where, slab, neighbour_shift, edge_coupling, cells, weight, reading, observation_variance, jitter)

    arrived = lax.all_to_all(pieces, LAG, 0, 0, tiled=True)

    def slot(age):
        return pl.BlockSpec((1, FIRST_ROWS, LANES), lambda i, o, *_: (o[age], 0, 0))

    sent = pl.pallas_call(
        select_kernel,
        grid_spec=pltpu.PrefetchScalarGridSpec(
            num_scalar_prefetch=1,
            grid=(1,),
            in_specs=[slot(0), whole(extra.shape)],
            out_specs=whole((spaces, SECOND_ROWS, LANES)),
        ),
        out_shape=jax.ShapeDtypeStruct((spaces, SECOND_ROWS, LANES), BF16),
        name="select",
    )(slot_order, arrived, extra)
    gathered = lax.all_to_all(sent, "space", 0, 0, tiled=True)

    sent = pl.pallas_call(
        observe_kernel,
        grid_spec=pltpu.PrefetchScalarGridSpec(
            num_scalar_prefetch=2,
            grid=(1,),
            in_specs=[whole(gathered.shape), slot(lags - 1), slot(lags - 2)],
            out_specs=pl.BlockSpec(memory_space=pl.ANY),
            scratch_shapes=[
                pltpu.VMEM((spaces, 40, LANES), F32),
                pltpu.VMEM((2, spaces, 32, LANES), BF16),
                pltpu.VMEM((THIRD_ROWS - 32, LANES), BF16),
                pltpu.VMEM((2, 32, LANES), BF16),
                pltpu.SemaphoreType.DMA((2, lags)),
            ],
        ),
        out_shape=jax.ShapeDtypeStruct((lags, THIRD_ROWS, LANES), BF16),
        name="observe",
    )(slot_order, where, gathered, arrived, arrived)
    gathered = lax.all_to_all(sent, LAG, 0, 0, tiled=True)

    return pl.pallas_call(
        analyse_kernel,
        grid_spec=pltpu.PrefetchScalarGridSpec(
            num_scalar_prefetch=2,
            grid=(1,),
            in_specs=[whole(gathered.shape), whole(slab_t.shape), whole(observation_variance.shape)],
            out_specs=[whole(ensemble.shape), whole((CYCLES, members // lags, LANES))],
            scratch_shapes=[pltpu.VMEM((members, LANES), F32)],
        ),
        out_shape=[
            jax.ShapeDtypeStruct(ensemble.shape, BF16),
            jax.ShapeDtypeStruct((CYCLES, members // lags, LANES), BF16),
        ],
        name="analyse",
    )(slot_order, where, gathered, slab_t, observation_variance)


def solution(mesh):
    split = Mesh(
        mesh.devices.reshape(4, 2, 4, mesh.shape["space"]), ("lag_0", "lag_1", "lag_2", "space")
    )
    placed = (
        P(LAG, "space", None),
        P(),
        P(None, "space"),
        P(None, "space"),
        P(None, None, "space"),
        P(None, None, "space"),
        P(None, "space"),
        P(),
        P(None, "space", None),
    )
    return jax.shard_map(
        on_device,
        mesh=split,
        in_specs=placed,
        out_specs=(P(LAG, "space", None), P(None, LAG, "space")),
        check_vma=False,
    )
```

```python
import jax
import jax.numpy as jnp
from jax import lax
from jax.experimental import pallas as pl
from jax.experimental.pallas import tpu as pltpu
from jax.sharding import Mesh
from jax.sharding import PartitionSpec as P

FC_STEPS = 4
CYCLES = 2
LAG = ("lag_0", "lag_1", "lag_2")
F32 = jnp.float32
BF16 = jnp.bfloat16
LANES = 128
FIRST_ROWS = 48
SECOND_ROWS = 96
THIRD = 5


def split3(x):
    hi = x.astype(BF16).astype(F32)
    mid = (x - hi).astype(BF16).astype(F32)
    low = (x - hi - mid).astype(BF16).astype(F32)
    return hi, mid, low


def to_bf16(x):
    return x.astype(BF16)


def ranks():
    return lax.axis_index(LAG), lax.axis_index("zh") * lax.axis_size("core") + lax.axis_index("core")


def prepare_kernel(
    slab, shift, coupling, cells, weight, reading, variance, jitter, slab_t, pieces, extra, tmp, wide
):
    values = slab[0].astype(F32)
    mean = jnp.mean(values, axis=1, keepdims=True)
    turned = values.T
    mean_row = jnp.broadcast_to(mean, (LANES, LANES)).T[0:8]
    hi, mid, low = split3(mean_row)
    row8 = lax.broadcasted_iota(jnp.int32, (8, LANES), 0)
    tail = jnp.where(row8 == 0, hi, jnp.where(row8 == 1, mid, jnp.where(row8 == 2, low, 0.0)))
    tail = to_bf16(jnp.concatenate([tail, jnp.zeros((8, LANES), F32)], axis=0))
    turned = to_bf16(turned)
    slab_t[...] = turned
    for r in range(32):
        pieces[r, 0:32, :] = turned[32 * r : 32 * r + 32]
        pieces[r, 32:48, :] = tail

    lag_rank, space_rank = ranks()
    near = pl.ds(pl.multiple_of(lag_rank // 4 * LANES, LANES), LANES)
    per = jitter.shape[1]
    noise = jnp.concatenate([jitter[0, :, near], jitter[1, :, near], jnp.zeros((96, LANES), F32)], axis=0)
    tmp[...] = noise.T
    noise = tmp[pl.ds(pl.multiple_of(32 * (lag_rank % 4), 32), 32), :]
    lane = lax.broadcasted_iota(jnp.int32, (32, LANES), 1)
    wide[...] = jnp.zeros_like(wide)
    for c in range(CYCLES):
        wide[4 * c : 4 * c + 4, 0:per] = cells[c].astype(F32)
        wide[8 + 4 * c : 12 + 4 * c, 0:per] = weight[c]
        wide[16 + 8 * c : 17 + 8 * c, 0:per] = reading[c : c + 1, :]
    back = lax.rem(LANES - per * space_rank, LANES)
    var = pltpu.roll(jnp.concatenate([variance[...]] * 4, axis=0), back, 1)
    var1 = pltpu.roll(var, per, 1)[1:2]
    var = jnp.where(lane[0:1] < per, var[0:1], jnp.where(lane[0:1] < 2 * per, var1, 0.0))
    read = (wide[16:24, :] + pltpu.roll(wide[24:32, :], per, 1))[0:1]
    error = read + jnp.sqrt(var) * noise
    hi, mid, low = split3(error)
    packed = jnp.where(
        lane < 32,
        hi,
        jnp.where(lane < 64, pltpu.roll(mid, 32, 1), jnp.where(lane < 96, pltpu.roll(low, 64, 1), 0.0)),
    )
    w_hi, w_mid, w_low = split3(wide[8:16, :])
    obs = jnp.concatenate([wide[0:8, :], w_hi, w_mid, w_low], axis=0)
    obs = pltpu.roll(obs, 96, 1)
    packed = jnp.where(lane < 96, packed, jnp.where(lane < 112, obs, 0.0))
    c_hi, c_mid, c_low = split3(coupling[...])
    extra[...] = to_bf16(jnp.concatenate([shift[...].astype(F32), c_hi, c_mid, c_low, packed], axis=0))


def select_kernel(order, arrived, extra, out):
    newest = arrived[order[0]].astype(F32)[0:40]
    piece = to_bf16(jnp.concatenate([newest, extra[...].astype(F32)], axis=0))
    for r in range(out.shape[0]):
        out[r] = piece


def mesh_rows(got, b):
    piece = got[b, 32:64, :].astype(F32)
    lane = lax.broadcasted_iota(jnp.int32, (1, LANES), 1)
    target = lane + piece[8:14].astype(jnp.int32)
    return target, piece[14:20] + piece[20:26] + piece[26:32]


def observation_rows(got, c):
    lane = lax.broadcasted_iota(jnp.int32, (32, LANES), 1)
    error = jnp.zeros((32, LANES), F32)
    obs = jnp.zeros((32, LANES), F32)
    for b in range(got.shape[0]):
        packed = got[b, 64:96, :].astype(F32)
        merged = packed + pltpu.roll(packed, 96, 1) + pltpu.roll(packed, 64, 1)
        mine = (lane >= 16 * b) & (lane < 16 * b + 16)
        error = jnp.where(mine, pltpu.roll(merged, (16 * b - 16 * c) % LANES, 1), error)
        obs = jnp.where(mine, pltpu.roll(packed, (16 * b + 32) % LANES, 1), obs)
    weight = obs[8:16] + obs[16:24] + obs[24:32]
    return error, obs[4 * c : 4 * c + 4].astype(jnp.int32), weight[4 * c : 4 * c + 4]


def build_mesh(got, matrix, total):
    row = lax.broadcasted_iota(jnp.int32, (LANES, LANES), 0)
    low, high = slice(0, 16), slice(LANES - 16, LANES)
    for b in range(got.shape[0]):
        target, weight = mesh_rows(got, b)
        inner = jnp.zeros((LANES, LANES), F32)
        before = jnp.zeros((16, LANES), F32)
        after = jnp.zeros((16, LANES), F32)
        every = jnp.zeros((1, LANES), F32)
        for k in range(6):
            goal = target[k : k + 1]
            at = goal & (LANES - 1)
            here = jnp.where(goal == at, weight[k : k + 1], 0.0)
            there = weight[k : k + 1] - here
            same = row == at
            inner = inner + jnp.where(same, here, 0.0)
            after = after + jnp.where(same[low], there, 0.0)
            before = before + jnp.where(same[high], there, 0.0)
            every = every + weight[k : k + 1]
        total[b] = jnp.broadcast_to(every, (8, LANES))
        edge = jnp.concatenate([after, jnp.zeros((LANES - 32, LANES), F32), before], axis=0)
        for at, part in ((0, inner), (LANES, edge)):
            hi = to_bf16(part)
            matrix[0, b, at : at + LANES, :] = hi
            matrix[1, b, at : at + LANES, :] = to_bf16(part - hi.astype(F32))


def relax(matrix, total, state):
    blocks = state.shape[0]
    lane = lax.broadcasted_iota(jnp.int32, (40, LANES), 1)

    def step(_, carry):
        now = [state[b] for b in range(blocks)]
        zero = jnp.zeros((40, LANES), F32)
        for b in range(blocks):
            before = now[b - 1] if b else zero
            after = now[b + 1] if b + 1 < blocks else zero
            beside = jnp.where(lane < 16, after, jnp.where(lane >= LANES - 16, before, 0.0))
            both = jnp.concatenate([now[b], beside], axis=1)
            hi = both.astype(BF16).astype(F32)
            wide = to_bf16(jnp.concatenate([hi, both - hi], axis=0))
            first = dot(wide, matrix[0, b])
            gain = first[0:40] + (first[40:80] + dot(wide[0:40], matrix[1, b]))
            state[b] = now[b] + (gain - total[b, 0:1, :] * now[b])
        return carry

    lax.fori_loop(0, FC_STEPS, step, 0)


def measure(values, cells, weight):
    lane = lax.broadcasted_iota(jnp.int32, (40, LANES), 1)
    total = jnp.zeros((40, LANES), F32)
    for q in range(4):
        index = jnp.broadcast_to(cells[q : q + 1], (40, LANES))
        picked = jnp.zeros((40, LANES), F32)
        for b, value in enumerate(values):
            mine = (lane >= 16 * b) & (lane < 16 * b + 16)
            picked = jnp.where(mine, jnp.take_along_axis(value, index, axis=1), picked)
        total = total + weight[q : q + 1] * picked
    return total


def observe_kernel(order, got, arrived, out, state, fields, matrix, total, common, own, sems):
    blocks = got.shape[0]
    lags = out.shape[0]
    fetch = [
        pltpu.make_async_copy(
            arrived.at[order[lags - 1 - i], pl.ds(0, 32), :], common.at[pl.ds(64 + 32 * i, 32), :], sems.at[2, i]
        )
        for i in range(2)
    ]
    for copy in fetch:
        copy.start()
    _, space_rank = ranks()
    core = lax.axis_index("core")
    build_mesh(got, matrix, total)
    for b in range(blocks):
        piece = got[b, 0:48, :].astype(F32)
        mean = piece[32:33] + piece[33:34] + piece[34:35]
        state[b] = jnp.concatenate([piece[0:32], jnp.broadcast_to(mean, (8, LANES))], axis=0)
    relax(matrix, total, state)
    forecast = []
    for b in range(blocks):
        value = state[b]
        rounded = to_bf16(value[0:32])
        fields[b] = rounded
        value = jnp.concatenate([rounded.astype(F32), value[32:40]], axis=0)
        state[b] = value
        forecast.append(value)
    own[0] = fields[space_rank]
    error, cells, weight = observation_rows(got, 0)
    seen = measure(forecast, cells, weight)
    spread = seen[0:32] - seen[32:33]
    innovation = error - seen[0:32]
    relax(matrix, total, state)
    own[1] = to_bf16(state[space_rank, 0:32, :])
    error, cells, weight = observation_rows(got, 1)
    seen = measure([state[b] for b in range(blocks)], cells, weight)
    common[0:32] = to_bf16(jnp.where(core == 0, spread, seen[0:32] - seen[32:33]))
    common[32:64] = to_bf16(jnp.where(core == 0, innovation, error - seen[0:32]))
    for copy in fetch:
        copy.wait()
    second = order[lags - 2]
    copies = []
    for r in range(lags):
        pick = jnp.where(second == r, 1, 0)
        copies.append(pltpu.make_async_copy(common, out.at[r, pl.ds(0, 128), :], sems.at[0, r]))
        copies.append(pltpu.make_async_copy(own.at[pick], out.at[r, pl.ds(128, 32), :], sems.at[1, r]))
    for copy in copies:
        copy.start()
    for copy in copies:
        copy.wait()


def run_next(jobs):
    for job in jobs[:2]:
        job()
    del jobs[:2]


def inverse(a, left, right, jobs):
    size = a.shape[0]
    lane = lax.broadcasted_iota(jnp.int32, (8, size), 1)
    tiles = [a[8 * r : 8 * r + 8] for r in range(size // 8)]
    for k in range(0, size, 4):
        t, o = k // 8, k % 8
        row = [jnp.broadcast_to(tiles[t][o + i : o + i + 1, :], (8, size)) for i in range(4)]
        d = [[jnp.broadcast_to(row[i][:, k + j : k + j + 1], (8, size)) for j in range(4)] for i in range(4)]
        pd = 1.0 / (d[0][0] * d[1][1] - d[0][1] * d[0][1])
        p00, p01, p11 = d[1][1] * pd, -d[0][1] * pd, d[0][0] * pd
        e00 = p00 * d[0][2] + p01 * d[1][2]
        e01 = p00 * d[0][3] + p01 * d[1][3]
        e10 = p01 * d[0][2] + p11 * d[1][2]
        e11 = p01 * d[0][3] + p11 * d[1][3]
        s00 = d[2][2] - (d[0][2] * e00 + d[1][2] * e10)
        s01 = d[2][3] - (d[0][2] * e01 + d[1][2] * e11)
        s11 = d[3][3] - (d[0][3] * e01 + d[1][3] * e11)
        sd = 1.0 / (s00 * s11 - s01 * s01)
        t00, t01, t11 = s11 * sd, -s01 * sd, s00 * sd
        g00 = e00 * t00 + e01 * t01
        g01 = e00 * t01 + e01 * t11
        g10 = e10 * t00 + e11 * t01
        g11 = e10 * t01 + e11 * t11
        off = p01 + g00 * e10 + g01 * e11
        inv = [
            [p00 + g00 * e00 + g01 * e01, off, -g00, -g01],
            [off, p11 + g10 * e10 + g11 * e11, -g10, -g11],
            [-g00, -g10, t00, t01],
            [-g01, -g11, t01, t11],
        ]
        scaled = []
        for i in range(4):
            z = inv[i][0] * row[0] + inv[i][1] * row[1] + inv[i][2] * row[2] + inv[i][3] * row[3]
            for j in range(4):
                z = jnp.where(lane == k + j, inv[i][j], z)
            scaled.append(z)
            left[k + i : k + i + 1, :] = jnp.where(lane < k, row[i], jnp.where(lane == k + i, 1.0, 0.0))[0:1]
            right[k + i : k + i + 1, :] = jnp.where(lane < k + 4, z, 0.0)[0:1]
        inside = (lane >= k) & (lane < k + 4)
        for r in range(t if o == 0 else t + 1, size // 8):
            old = tiles[r]
            new = jnp.where(inside, 0.0, old)
            for i in range(4):
                new = new - jnp.broadcast_to(old[:, k + i : k + i + 1], (8, size)) * scaled[i]
            tiles[r] = new
        run_next(jobs)
    while jobs:
        run_next(jobs)
    return lax.dot_general(
        left[...].T,
        right[...],
        (((1,), (0,)), ((), ())),
        precision=lax.Precision.HIGHEST,
        preferred_element_type=F32,
    )


def dot(a, b):
    return lax.dot_general(a, b, (((1,), (0,)), ((), ())), preferred_element_type=F32)


def centred(values):
    return to_bf16(values - jnp.mean(values, axis=0, keepdims=True))


def solve(innovation, inverse_gram):
    hi, mid, low = split3(inverse_gram)
    total = dot(innovation, to_bf16(hi)) + (dot(innovation, to_bf16(mid)) + dot(innovation, to_bf16(low)))
    return to_bf16(total)


def eye():
    rows = lax.broadcasted_iota(jnp.int32, (LANES, LANES), 0)
    return rows == lax.broadcasted_iota(jnp.int32, (LANES, LANES), 1)


def turned(values):
    return values.astype(F32).T.astype(BF16)


def gram_of(spread, spread_t, variance):
    scale = spread_t.shape[0] - 1
    return dot(spread, spread_t) + jnp.where(eye(), scale * variance, 0.0)


def put_gain(gain, i, spread, values):
    product = dot(spread, values)
    hi = to_bf16(product)
    gain[i, 0] = hi
    gain[i, 1] = to_bf16(product - hi.astype(F32))


def change(gain, i, rows):
    return dot(rows, gain[i, 0]) + dot(rows, gain[i, 1])


def analyse_kernel(
    order, got, other, slab_t, variance, analysed, retired, parts, now, cent, gain, left, right, solved, sems
):
    lags = got.shape[0]
    lag_rank, _ = ranks()
    members = slab_t.shape[0]
    block = members // lags
    mine = pl.ds(pl.multiple_of(lag_rank * block, block), block)
    own_core = lax.axis_index("core")

    def copy_of(source, i, to):
        return pltpu.make_async_copy(source.at[:, pl.ds(block * i, block), :], parts.at[to], sems.at[to])

    for i in range(2):
        for core in range(2):

            @pl.when(own_core == core)
            def _():
                copy_of(got, i, 2 * core + i).start()
                copy_of(other, i, 2 * (1 - core) + i).start()

    for i in range(3):
        copy_of(got, 2 + i, 4 + i).start()

    def wait(i):
        copy_of(got, 0, i).wait()

    def part(i):
        return parts[i].reshape(members, LANES)

    chunks = [slice(LANES * c, LANES * c + LANES) for c in range(members // LANES)]
    took = (lag_rank == order[lags - 1]) | (lag_rank == order[lags - 2])

    def folded(values):
        return values.reshape(values.shape[0] // 8, 8, LANES).sum(axis=0)

    def centre_jobs(i, load):
        sums = []
        kept = []

        def look(rows):
            def job():
                sums.append(folded(load(rows).astype(F32)))

            return job

        def centre(rows):
            def job():
                if not kept:
                    total = sum(sums[1:], sums[0])
                    kept.append(jnp.sum(total, axis=0, keepdims=True) * (1.0 / members))
                cent[i, rows, :] = to_bf16(now[i, rows, :].astype(F32) - kept[0])

            return job

        return [look(rows) for rows in chunks] + [centre(rows) for rows in chunks]

    def gain_job(i, spread, values):
        return lambda: put_gain(gain, i, spread, values())

    wait(0)
    spread = turned(part(0))
    gram = gram_of(spread, part(0), variance[0:1, :])
    for i in range(1, 7):
        wait(i)

    def keep(i, load):
        def loaded(rows):
            values = load(rows)
            now[i, rows, :] = values
            return values

        return loaded

    def rows_of(i, rows):
        return parts[i, rows.start // block : rows.stop // block].reshape(LANES, LANES)

    jobs = [gain_job(3, spread, lambda: part(2))]
    jobs += centre_jobs(0, keep(0, lambda rows: jnp.where(took, rows_of(6, rows), slab_t[rows, :])))
    jobs += [gain_job(0, spread, lambda: cent[0])]
    jobs += centre_jobs(1, keep(1, lambda rows: rows_of(5, rows)))
    jobs += [gain_job(1, spread, lambda: cent[1])]
    jobs += centre_jobs(2, keep(2, lambda rows: rows_of(4, rows)))
    jobs += [gain_job(2, spread, lambda: cent[2])]
    solved[...] = solve(part(1), inverse(gram, left, right, jobs))
    seen = change(gain, 3, solved[...])
    spread_t = centred(part(2).astype(F32) + seen)
    innovation = to_bf16(part(3).astype(F32) - seen)
    spread = turned(spread_t)
    gram = gram_of(spread, spread_t, variance[1:2, :])

    def renewed(i):
        def load(rows):
            values = to_bf16(now[i, rows, :].astype(F32) + change(gain, i, solved[rows, :]))
            now[i, rows, :] = values
            return values

        return load

    def retire_first():
        retired[0] = to_bf16(now[2, mine, :].astype(F32) + change(gain, 2, solved[mine, :]))

    jobs = centre_jobs(0, renewed(0)) + centre_jobs(1, renewed(1)) + [retire_first]
    jobs += [gain_job(0, spread, lambda: cent[0]), gain_job(1, spread, lambda: cent[1])]
    solved_again = solve(innovation, inverse(gram, left, right, jobs))
    analysed[0] = to_bf16((now[0].astype(F32) + change(gain, 0, solved_again)).T)
    solved[...] = solved_again
    retired[1] = to_bf16(now[1, mine, :].astype(F32) + change(gain, 1, solved[mine, :]))


def whole(shape):
    return pl.BlockSpec(shape, lambda i, *_: (0,) * len(shape))


def on_device(
    ensemble,
    slot_order,
    neighbour_shift,
    edge_coupling,
    observation_cells,
    observation_weight,
    observation_reading,
    observation_variance,
    observation_jitter,
):
    lags = lax.axis_size(LAG)
    spaces = lax.axis_size("zh") * lax.axis_size("core")
    per = observation_reading.shape[1]
    members = ensemble.shape[2]

    inputs = (
        ensemble,
        neighbour_shift,
        edge_coupling,
        observation_cells,
        observation_weight,
        observation_reading,
        observation_variance,
        observation_jitter,
    )
    slab_t, pieces, extra = pl.pallas_call(
        prepare_kernel,
        out_shape=[
            jax.ShapeDtypeStruct((members, LANES), BF16),
            jax.ShapeDtypeStruct((lags, FIRST_ROWS, LANES), BF16),
            jax.ShapeDtypeStruct((SECOND_ROWS - 40, LANES), BF16),
        ],
        scratch_shapes=[pltpu.VMEM((LANES, LANES), F32), pltpu.VMEM((32, LANES), F32)],
        name="prepare",
    )(*inputs)

    arrived = lax.all_to_all(pieces, LAG, 0, 0, tiled=True)

    vmem = pl.BlockSpec(memory_space=pltpu.VMEM)
    smem = pl.BlockSpec(memory_space=pltpu.SMEM)
    away = pl.BlockSpec(memory_space=pl.ANY)
    sent = pl.pallas_call(
        select_kernel,
        in_specs=[smem, vmem, vmem],
        out_specs=vmem,
        out_shape=jax.ShapeDtypeStruct((spaces, SECOND_ROWS, LANES), BF16),
        name="select",
    )(slot_order, arrived, extra)
    gathered = lax.all_to_all(sent, ("zh", "core"), 0, 0, tiled=True)

    block = members // lags
    sent = pl.pallas_call(
        observe_kernel,
        in_specs=[smem, vmem, away],
        out_specs=away,
        out_shape=jax.ShapeDtypeStruct((lags, THIRD * block, LANES), BF16),
        scratch_shapes=[
            pltpu.VMEM((spaces, 40, LANES), F32),
            pltpu.VMEM((spaces, block, LANES), BF16),
            pltpu.VMEM((2, spaces, 2 * LANES, LANES), BF16),
            pltpu.VMEM((spaces, 8, LANES), F32),
            pltpu.VMEM(((THIRD - 1) * block, LANES), BF16),
            pltpu.VMEM((2, block, LANES), BF16),
            pltpu.SemaphoreType.DMA((3, lags)),
        ],
        name="observe",
    )(slot_order, gathered, arrived)
    third = lax.all_to_all(sent, LAG, 0, 0, tiled=True)
    other = lax.ppermute(third[:, 0 : 2 * block], "core", [(0, 1), (1, 0)])

    square = pltpu.VMEM((LANES, LANES), F32)
    return pl.pallas_call(
        analyse_kernel,
        in_specs=[smem, away, away, vmem, vmem],
        out_specs=[vmem, vmem],
        out_shape=[
            jax.ShapeDtypeStruct(ensemble.shape, BF16),
            jax.ShapeDtypeStruct((CYCLES, block, LANES), BF16),
        ],
        scratch_shapes=[
            pltpu.VMEM((THIRD + 2, lags, block, LANES), BF16),
            pltpu.VMEM((3, members, LANES), BF16),
            pltpu.VMEM((3, members, LANES), BF16),
            pltpu.VMEM((4, 2, LANES, LANES), BF16),
            square,
            square,
            pltpu.VMEM((members, LANES), BF16),
            pltpu.SemaphoreType.DMA((THIRD + 2,)),
        ],
        name="analyse",
    )(slot_order, third, other, slab_t, observation_variance)


def solution(mesh):
    split = Mesh(
        mesh.devices.reshape(4, 2, 4, mesh.shape["space"] // 2, 2), LAG + ("zh", "core")
    )
    space = ("zh", "core")
    placed = (
        P(LAG, space, None),
        P(),
        P(None, space),
        P(None, space),
        P(None, None, space),
        P(None, None, space),
        P(None, space),
        P(),
        P(None, space, None),
    )
    return jax.shard_map(
        on_device,
        mesh=split,
        in_specs=placed,
        out_specs=(P(LAG, space, None), P(None, LAG, space)),
        check_vma=False,
    )
```

```python
import jax
import jax.numpy as jnp
from jax import lax
from jax.experimental import pallas as pl
from jax.experimental.pallas import tpu as pltpu
from jax.sharding import Mesh
from jax.sharding import PartitionSpec as P

FC_STEPS = 4
CYCLES = 2
LAG = ("lag_0", "lag_1", "lag_2")
F32 = jnp.float32
BF16 = jnp.bfloat16
LANES = 128
FIRST_ROWS = 48
SECOND_ROWS = 96
THIRD = 5


def split3(x):
    hi = x.astype(BF16).astype(F32)
    mid = (x - hi).astype(BF16).astype(F32)
    low = (x - hi - mid).astype(BF16).astype(F32)
    return hi, mid, low


def to_bf16(x):
    return x.astype(BF16)


def ranks():
    return lax.axis_index(LAG), lax.axis_index("zh") * lax.axis_size("core") + lax.axis_index("core")


def prepare_kernel(
    slab, shift, coupling, cells, weight, reading, variance, jitter, slab_t, pieces, extra, tmp, wide
):
    values = slab[0].astype(F32)
    mean = jnp.mean(values, axis=1, keepdims=True)
    turned = values.T
    mean_row = jnp.broadcast_to(mean, (LANES, LANES)).T[0:8]
    hi, mid, low = split3(mean_row)
    row8 = lax.broadcasted_iota(jnp.int32, (8, LANES), 0)
    tail = jnp.where(row8 == 0, hi, jnp.where(row8 == 1, mid, jnp.where(row8 == 2, low, 0.0)))
    tail = to_bf16(jnp.concatenate([tail, jnp.zeros((8, LANES), F32)], axis=0))
    turned = to_bf16(turned)
    slab_t[...] = turned
    for r in range(32):
        pieces[r, 0:32, :] = turned[32 * r : 32 * r + 32]
        pieces[r, 32:48, :] = tail

    lag_rank, space_rank = ranks()
    near = pl.ds(pl.multiple_of(lag_rank // 4 * LANES, LANES), LANES)
    per = jitter.shape[1]
    noise = jnp.concatenate([jitter[0, :, near], jitter[1, :, near], jnp.zeros((96, LANES), F32)], axis=0)
    tmp[...] = noise.T
    noise = tmp[pl.ds(pl.multiple_of(32 * (lag_rank % 4), 32), 32), :]
    lane = lax.broadcasted_iota(jnp.int32, (32, LANES), 1)
    wide[...] = jnp.zeros_like(wide)
    for c in range(CYCLES):
        wide[4 * c : 4 * c + 4, 0:per] = cells[c].astype(F32)
        wide[8 + 4 * c : 12 + 4 * c, 0:per] = weight[c]
        wide[16 + 8 * c : 17 + 8 * c, 0:per] = reading[c : c + 1, :]
    back = lax.rem(LANES - per * space_rank, LANES)
    var = pltpu.roll(jnp.concatenate([variance[...]] * 4, axis=0), back, 1)
    var1 = pltpu.roll(var, per, 1)[1:2]
    var = jnp.where(lane[0:1] < per, var[0:1], jnp.where(lane[0:1] < 2 * per, var1, 0.0))
    read = (wide[16:24, :] + pltpu.roll(wide[24:32, :], per, 1))[0:1]
    error = read + jnp.sqrt(var) * noise
    hi, mid, low = split3(error)
    packed = jnp.where(
        lane < 32,
        hi,
        jnp.where(lane < 64, pltpu.roll(mid, 32, 1), jnp.where(lane < 96, pltpu.roll(low, 64, 1), 0.0)),
    )
    w_hi, w_mid, w_low = split3(wide[8:16, :])
    obs = jnp.concatenate([wide[0:8, :], w_hi, w_mid, w_low], axis=0)
    obs = pltpu.roll(obs, 96, 1)
    packed = jnp.where(lane < 96, packed, jnp.where(lane < 112, obs, 0.0))
    c_hi, c_mid, c_low = split3(coupling[...])
    extra[...] = to_bf16(jnp.concatenate([shift[...].astype(F32), c_hi, c_mid, c_low, packed], axis=0))


def select_kernel(order, arrived, extra, out):
    newest = arrived[order[0]].astype(F32)[0:40]
    piece = to_bf16(jnp.concatenate([newest, extra[...].astype(F32)], axis=0))
    for r in range(out.shape[0]):
        out[r] = piece


def mesh_rows(got, b):
    piece = got[b, 32:64, :].astype(F32)
    lane = lax.broadcasted_iota(jnp.int32, (1, LANES), 1)
    target = lane + piece[8:14].astype(jnp.int32)
    return target, piece[14:20] + piece[20:26] + piece[26:32]


def observation_rows(got, c):
    lane = lax.broadcasted_iota(jnp.int32, (32, LANES), 1)
    error = jnp.zeros((32, LANES), F32)
    obs = jnp.zeros((32, LANES), F32)
    for b in range(got.shape[0]):
        packed = got[b, 64:96, :].astype(F32)
        merged = packed + pltpu.roll(packed, 96, 1) + pltpu.roll(packed, 64, 1)
        mine = (lane >= 16 * b) & (lane < 16 * b + 16)
        error = jnp.where(mine, pltpu.roll(merged, (16 * b - 16 * c) % LANES, 1), error)
        obs = jnp.where(mine, pltpu.roll(packed, (16 * b + 32) % LANES, 1), obs)
    weight = obs[8:16] + obs[16:24] + obs[24:32]
    return error, obs[4 * c : 4 * c + 4].astype(jnp.int32), weight[4 * c : 4 * c + 4]


def build_mesh(got, matrix, total):
    row = lax.broadcasted_iota(jnp.int32, (LANES, LANES), 0)
    low, high = slice(0, 16), slice(LANES - 16, LANES)
    for b in range(got.shape[0]):
        target, weight = mesh_rows(got, b)
        inner = jnp.zeros((LANES, LANES), F32)
        before = jnp.zeros((16, LANES), F32)
        after = jnp.zeros((16, LANES), F32)
        every = jnp.zeros((1, LANES), F32)
        for k in range(6):
            goal = target[k : k + 1]
            at = goal & (LANES - 1)
            here = jnp.where(goal == at, weight[k : k + 1], 0.0)
            there = weight[k : k + 1] - here
            same = row == at
            inner = inner + jnp.where(same, here, 0.0)
            after = after + jnp.where(same[low], there, 0.0)
            before = before + jnp.where(same[high], there, 0.0)
            every = every + weight[k : k + 1]
        total[b] = jnp.broadcast_to(every, (8, LANES))
        edge = jnp.concatenate([after, jnp.zeros((LANES - 32, LANES), F32), before], axis=0)
        for at, part in ((0, inner), (LANES, edge)):
            hi = to_bf16(part)
            matrix[0, b, at : at + LANES, :] = hi
            matrix[1, b, at : at + LANES, :] = to_bf16(part - hi.astype(F32))


def relax(matrix, total, state):
    blocks = state.shape[0]
    lane = lax.broadcasted_iota(jnp.int32, (40, LANES), 1)

    def step(_, carry):
        now = [state[b] for b in range(blocks)]
        zero = jnp.zeros((40, LANES), F32)
        for b in range(blocks):
            before = now[b - 1] if b else zero
            after = now[b + 1] if b + 1 < blocks else zero
            beside = jnp.where(lane < 16, after, jnp.where(lane >= LANES - 16, before, 0.0))
            both = jnp.concatenate([now[b], beside], axis=1)
            hi = both.astype(BF16).astype(F32)
            wide = to_bf16(jnp.concatenate([hi, both - hi], axis=0))
            first = dot(wide, matrix[0, b])
            gain = first[0:40] + (first[40:80] + dot(wide[0:40], matrix[1, b]))
            state[b] = now[b] + (gain - total[b, 0:1, :] * now[b])
        return carry

    lax.fori_loop(0, FC_STEPS, step, 0)


def measure(values, cells, weight):
    lane = lax.broadcasted_iota(jnp.int32, (40, LANES), 1)
    total = jnp.zeros((40, LANES), F32)
    for q in range(4):
        index = jnp.broadcast_to(cells[q : q + 1], (40, LANES))
        picked = jnp.zeros((40, LANES), F32)
        for b, value in enumerate(values):
            mine = (lane >= 16 * b) & (lane < 16 * b + 16)
            picked = jnp.where(mine, jnp.take_along_axis(value, index, axis=1), picked)
        total = total + weight[q : q + 1] * picked
    return total


def observe_kernel(order, one, two, arrived, out, got, state, fields, matrix, total, common, own, sems):
    blocks = got.shape[0]
    lags = out.shape[0]
    fetch = [
        pltpu.make_async_copy(
            arrived.at[order[lags - 1 - i], pl.ds(0, 32), :], common.at[pl.ds(64 + 32 * i, 32), :], sems.at[2, i]
        )
        for i in range(2)
    ]
    for copy in fetch:
        copy.start()
    _, space_rank = ranks()
    core = lax.axis_index("core")
    for z in range(one.shape[0]):
        got[2 * z + core] = one[z]
        got[2 * z + 1 - core] = two[z]
    build_mesh(got, matrix, total)
    for b in range(blocks):
        piece = got[b, 0:48, :].astype(F32)
        mean = piece[32:33] + piece[33:34] + piece[34:35]
        state[b] = jnp.concatenate([piece[0:32], jnp.broadcast_to(mean, (8, LANES))], axis=0)
    relax(matrix, total, state)
    forecast = []
    for b in range(blocks):
        value = state[b]
        rounded = to_bf16(value[0:32])
        fields[b] = rounded
        value = jnp.concatenate([rounded.astype(F32), value[32:40]], axis=0)
        state[b] = value
        forecast.append(value)
    own[0] = fields[space_rank]
    error, cells, weight = observation_rows(got, 0)
    seen = measure(forecast, cells, weight)
    spread = seen[0:32] - seen[32:33]
    innovation = error - seen[0:32]
    relax(matrix, total, state)
    own[1] = to_bf16(state[space_rank, 0:32, :])
    error, cells, weight = observation_rows(got, 1)
    seen = measure([state[b] for b in range(blocks)], cells, weight)
    common[0:32] = to_bf16(jnp.where(core == 0, spread, seen[0:32] - seen[32:33]))
    common[32:64] = to_bf16(jnp.where(core == 0, innovation, error - seen[0:32]))
    for copy in fetch:
        copy.wait()
    second = order[lags - 2]
    copies = []
    for r in range(lags):
        pick = jnp.where(second == r, 1, 0)
        copies.append(pltpu.make_async_copy(common, out.at[r, pl.ds(0, 128), :], sems.at[0, r]))
        copies.append(pltpu.make_async_copy(own.at[pick], out.at[r, pl.ds(128, 32), :], sems.at[1, r]))
    for copy in copies:
        copy.start()
    for copy in copies:
        copy.wait()


def run_next(jobs):
    for job in jobs[:2]:
        job()
    del jobs[:2]


def eliminate(d):
    pd = 1.0 / (d[0][0] * d[1][1] - d[0][1] * d[0][1])
    p00, p01, p11 = d[1][1] * pd, -d[0][1] * pd, d[0][0] * pd
    e00 = p00 * d[0][2] + p01 * d[1][2]
    e01 = p00 * d[0][3] + p01 * d[1][3]
    e10 = p01 * d[0][2] + p11 * d[1][2]
    e11 = p01 * d[0][3] + p11 * d[1][3]
    s00 = d[2][2] - (d[0][2] * e00 + d[1][2] * e10)
    s01 = d[2][3] - (d[0][2] * e01 + d[1][2] * e11)
    s11 = d[3][3] - (d[0][3] * e01 + d[1][3] * e11)
    sd = 1.0 / (s00 * s11 - s01 * s01)

    def apply(m):
        y0 = p00 * m[0] + p01 * m[1]
        y1 = p01 * m[0] + p11 * m[1]
        y2 = m[2] - (d[0][2] * y0 + d[1][2] * y1)
        y3 = m[3] - (d[0][3] * y0 + d[1][3] * y1)
        z2 = (s11 * y2 - s01 * y3) * sd
        z3 = (s00 * y3 - s01 * y2) * sd
        return [y0 - (e00 * z2 + e01 * z3), y1 - (e10 * z2 + e11 * z3), z2, z3]

    return apply


def product4(c, z):
    return (c[0] * z[0] + c[1] * z[1]) + (c[2] * z[2] + c[3] * z[3])


def inverse(a, left, right, jobs):
    size = a.shape[0]
    lane = lax.broadcasted_iota(jnp.int32, (8, size), 1)
    tiles = [a[8 * r : 8 * r + 8] for r in range(size // 8)]

    def rows4(tile, o):
        return [jnp.broadcast_to(tile[o + i : o + i + 1, :], (8, size)) for i in range(4)]

    def put(row, k, scaled):
        for i in range(4):
            unit = jnp.where(lane == k + i, 1.0, 0.0)
            left[k + i : k + i + 1, :] = jnp.where(lane < k, row[i], unit)[0:1]
            right[k + i : k + i + 1, :] = jnp.where(lane < k + 4, scaled[i], 0.0)[0:1]

    for t in range(size // 8):
        k = 8 * t
        columns = [
            [jnp.broadcast_to(tiles[r][:, k + j : k + j + 1], (8, size)) for j in range(8)]
            for r in range(t, size // 8)
        ]
        first = (lane >= k) & (lane < k + 4)
        second = (lane >= k + 4) & (lane < k + 8)
        row = rows4(tiles[t], 0)
        d = [rows4(column, 0) for column in columns[0]]
        d = [[d[j][i] for j in range(8)] for i in range(4)]
        apply = eliminate(d)
        scaled = apply([jnp.where(first, jnp.where(lane == k + i, 1.0, 0.0), row[i]) for i in range(4)])
        ahead = [apply([d[i][4 + j] for i in range(4)]) for j in range(4)]
        put(row, k, scaled)
        updated = []
        for r in range(t, size // 8):
            c = columns[r - t]
            tiles[r] = jnp.where(first, 0.0, tiles[r]) - product4(c, scaled)
            updated.append([c[4 + j] - product4(c, ahead[j]) for j in range(4)])
        run_next(jobs)
        row = rows4(tiles[t], 4)
        d = [rows4(column, 4) for column in updated[0]]
        d = [[d[j][i] for j in range(4)] for i in range(4)]
        apply = eliminate(d)
        scaled = apply([jnp.where(second, jnp.where(lane == k + 4 + i, 1.0, 0.0), row[i]) for i in range(4)])
        put(row, k + 4, scaled)
        for r in range(t + 1, size // 8):
            tiles[r] = jnp.where(second, 0.0, tiles[r]) - product4(updated[r - t], scaled)
        run_next(jobs)
    while jobs:
        run_next(jobs)
    return lax.dot_general(
        left[...].T,
        right[...],
        (((1,), (0,)), ((), ())),
        precision=lax.Precision.HIGHEST,
        preferred_element_type=F32,
    )


def dot(a, b):
    return lax.dot_general(a, b, (((1,), (0,)), ((), ())), preferred_element_type=F32)


def centred(values):
    return to_bf16(values - jnp.mean(values, axis=0, keepdims=True))


def stacked(values):
    hi = to_bf16(values)
    return jnp.concatenate([hi, to_bf16(values - hi.astype(F32))], axis=0)


def doubled(values):
    return jnp.concatenate([values, values], axis=1)


def eye():
    rows = lax.broadcasted_iota(jnp.int32, (LANES, LANES), 0)
    return rows == lax.broadcasted_iota(jnp.int32, (LANES, LANES), 1)


def turned(values):
    return values.astype(F32).T.astype(BF16)


def gram_of(spread, spread_t, variance):
    scale = spread_t.shape[0] - 1
    return dot(spread, spread_t) + jnp.where(eye(), scale * variance, 0.0)


def put_gain(gain, i, spread, values):
    gain[i] = stacked(dot(spread, values))


def change(gain, i, rows):
    return dot(rows, gain[i])


def analyse_kernel(
    order, got, other, slab_t, variance, analysed, retired, parts, now, cent, gain, left, right, solved, sems
):
    lags = got.shape[0]
    lag_rank, _ = ranks()
    members = slab_t.shape[0]
    block = members // lags
    mine = pl.ds(pl.multiple_of(lag_rank * block, block), block)
    own_core = lax.axis_index("core")

    def copy_of(source, i, to):
        return pltpu.make_async_copy(source.at[:, pl.ds(block * i, block), :], parts.at[to], sems.at[to])

    for i in range(2):
        for core in range(2):

            @pl.when(own_core == core)
            def _():
                copy_of(got, i, 2 * core + i).start()
                copy_of(other, i, 2 * (1 - core) + i).start()

    for i in range(3):
        copy_of(got, 2 + i, 4 + i).start()

    def wait(i):
        copy_of(got, 0, i).wait()

    def part(i):
        return parts[i].reshape(members, LANES)

    chunks = [slice(LANES * c, LANES * c + LANES) for c in range(members // LANES)]
    took = (lag_rank == order[lags - 1]) | (lag_rank == order[lags - 2])

    def folded(values):
        return values.reshape(values.shape[0] // 8, 8, LANES).sum(axis=0)

    def centre_jobs(i, load):
        sums = []
        kept = []

        def look(rows):
            def job():
                sums.append(folded(load(rows).astype(F32)))

            return job

        def centre(rows):
            def job():
                if not kept:
                    total = sum(sums[1:], sums[0])
                    kept.append(jnp.sum(total, axis=0, keepdims=True) * (1.0 / members))
                cent[i, rows, :] = to_bf16(now[i, rows, :].astype(F32) - kept[0])

            return job

        return [look(rows) for rows in chunks] + [centre(rows) for rows in chunks]

    def gain_job(i, spread, values):
        return lambda: put_gain(gain, i, spread, values())

    wait(0)
    spread = turned(part(0))
    gram = gram_of(spread, part(0), variance[0:1, :])
    for i in range(1, 7):
        wait(i)

    def keep(i, load):
        def loaded(rows):
            values = load(rows)
            now[i, rows, :] = values
            return values

        return loaded

    def rows_of(i, rows):
        return parts[i, rows.start // block : rows.stop // block].reshape(LANES, LANES)

    jobs = [gain_job(3, spread, lambda: part(2))]
    jobs += centre_jobs(0, keep(0, lambda rows: jnp.where(took, rows_of(6, rows), slab_t[rows, :])))
    jobs += [gain_job(0, spread, lambda: cent[0])]
    jobs += centre_jobs(1, keep(1, lambda rows: rows_of(5, rows)))
    jobs += [gain_job(1, spread, lambda: cent[1])]
    jobs += centre_jobs(2, keep(2, lambda rows: rows_of(4, rows)))
    jobs += [gain_job(2, spread, lambda: cent[2])]
    solved[...] = doubled(to_bf16(dot(doubled(part(1)), stacked(inverse(gram, left, right, jobs)))))
    seen = change(gain, 3, solved[...])
    spread_t = centred(part(2).astype(F32) + seen)
    innovation = to_bf16(part(3).astype(F32) - seen)
    spread = turned(spread_t)
    gram = gram_of(spread, spread_t, variance[1:2, :])

    def renewed(i):
        def load(rows):
            values = to_bf16(now[i, rows, :].astype(F32) + change(gain, i, solved[rows, :]))
            now[i, rows, :] = values
            return values

        return load

    def retire_first():
        retired[0] = to_bf16(now[2, mine, :].astype(F32) + change(gain, 2, solved[mine, :]))

    jobs = centre_jobs(0, renewed(0)) + centre_jobs(1, renewed(1)) + [retire_first]
    jobs += [gain_job(0, spread, lambda: cent[0]), gain_job(1, spread, lambda: cent[1])]
    solved_again = doubled(to_bf16(dot(doubled(innovation), stacked(inverse(gram, left, right, jobs)))))
    analysed[0] = to_bf16((now[0].astype(F32) + change(gain, 0, solved_again)).T)
    solved[...] = solved_again
    retired[1] = to_bf16(now[1, mine, :].astype(F32) + change(gain, 1, solved[mine, :]))


def whole(shape):
    return pl.BlockSpec(shape, lambda i, *_: (0,) * len(shape))


def on_device(
    ensemble,
    slot_order,
    neighbour_shift,
    edge_coupling,
    observation_cells,
    observation_weight,
    observation_reading,
    observation_variance,
    observation_jitter,
):
    lags = lax.axis_size(LAG)
    spaces = lax.axis_size("zh") * lax.axis_size("core")
    per = observation_reading.shape[1]
    members = ensemble.shape[2]

    inputs = (
        ensemble,
        neighbour_shift,
        edge_coupling,
        observation_cells,
        observation_weight,
        observation_reading,
        observation_variance,
        observation_jitter,
    )
    slab_t, pieces, extra = pl.pallas_call(
        prepare_kernel,
        out_shape=[
            jax.ShapeDtypeStruct((members, LANES), BF16),
            jax.ShapeDtypeStruct((lags, FIRST_ROWS, LANES), BF16),
            jax.ShapeDtypeStruct((SECOND_ROWS - 40, LANES), BF16),
        ],
        scratch_shapes=[pltpu.VMEM((LANES, LANES), F32), pltpu.VMEM((32, LANES), F32)],
        name="prepare",
    )(*inputs)

    arrived = lax.all_to_all(pieces, LAG, 0, 0, tiled=True)

    vmem = pl.BlockSpec(memory_space=pltpu.VMEM)
    smem = pl.BlockSpec(memory_space=pltpu.SMEM)
    away = pl.BlockSpec(memory_space=pl.ANY)
    sent = pl.pallas_call(
        select_kernel,
        in_specs=[smem, vmem, vmem],
        out_specs=vmem,
        out_shape=jax.ShapeDtypeStruct((spaces // 2, SECOND_ROWS, LANES), BF16),
        name="select",
    )(slot_order, arrived, extra)
    gathered = lax.all_to_all(sent, "zh", 0, 0, tiled=True)
    swapped = lax.ppermute(gathered, "core", [(0, 1), (1, 0)])

    block = members // lags
    sent = pl.pallas_call(
        observe_kernel,
        in_specs=[smem, vmem, vmem, away],
        out_specs=away,
        out_shape=jax.ShapeDtypeStruct((lags, THIRD * block, LANES), BF16),
        scratch_shapes=[
            pltpu.VMEM((spaces, SECOND_ROWS, LANES), BF16),
            pltpu.VMEM((spaces, 40, LANES), F32),
            pltpu.VMEM((spaces, block, LANES), BF16),
            pltpu.VMEM((2, spaces, 2 * LANES, LANES), BF16),
            pltpu.VMEM((spaces, 8, LANES), F32),
            pltpu.VMEM(((THIRD - 1) * block, LANES), BF16),
            pltpu.VMEM((2, block, LANES), BF16),
            pltpu.SemaphoreType.DMA((3, lags)),
        ],
        name="observe",
    )(slot_order, gathered, swapped, arrived)
    third = lax.all_to_all(sent, LAG, 0, 0, tiled=True)
    other = lax.ppermute(third[:, 0 : 2 * block], "core", [(0, 1), (1, 0)])

    square = pltpu.VMEM((LANES, LANES), F32)
    return pl.pallas_call(
        analyse_kernel,
        in_specs=[smem, away, away, vmem, vmem],
        out_specs=[vmem, vmem],
        out_shape=[
            jax.ShapeDtypeStruct(ensemble.shape, BF16),
            jax.ShapeDtypeStruct((CYCLES, block, LANES), BF16),
        ],
        scratch_shapes=[
            pltpu.VMEM((THIRD + 2, lags, block, LANES), BF16),
            pltpu.VMEM((3, members, LANES), BF16),
            pltpu.VMEM((3, members, LANES), BF16),
            pltpu.VMEM((4, 2 * LANES, LANES), BF16),
            square,
            square,
            pltpu.VMEM((members, 2 * LANES), BF16),
            pltpu.SemaphoreType.DMA((THIRD + 2,)),
        ],
        name="analyse",
    )(slot_order, third, other, slab_t, observation_variance)


def solution(mesh):
    split = Mesh(
        mesh.devices.reshape(4, 2, 4, mesh.shape["space"] // 2, 2), LAG + ("zh", "core")
    )
    space = ("zh", "core")
    placed = (
        P(LAG, space, None),
        P(),
        P(None, space),
        P(None, space),
        P(None, None, space),
        P(None, None, space),
        P(None, space),
        P(),
        P(None, space, None),
    )
    return jax.shard_map(
        on_device,
        mesh=split,
        in_specs=placed,
        out_specs=(P(LAG, space, None), P(None, LAG, space)),
        check_vma=False,
    )
```

```python
import jax
import jax.numpy as jnp
from jax import lax
from jax.experimental import pallas as pl
from jax.experimental.pallas import tpu as pltpu
from jax.sharding import Mesh
from jax.sharding import PartitionSpec as P

FC_STEPS = 4
CYCLES = 2
LAG = ("lag_0", "lag_1", "lag_2")
F32 = jnp.float32
BF16 = jnp.bfloat16
LANES = 128
FIRST_ROWS = 48
SECOND_ROWS = 96
THIRD = 4


def split3(x):
    hi = x.astype(BF16).astype(F32)
    mid = (x - hi).astype(BF16).astype(F32)
    low = (x - hi - mid).astype(BF16).astype(F32)
    return hi, mid, low


def to_bf16(x):
    return x.astype(BF16)


def ranks():
    return lax.axis_index(LAG), lax.axis_index("zh") * lax.axis_size("core") + lax.axis_index("core")


def prepare_kernel(
    slab, shift, coupling, cells, weight, reading, variance, jitter, slab_t, pieces, extra, tmp, wide
):
    values = slab[0].astype(F32)
    mean = jnp.mean(values, axis=1, keepdims=True)
    turned = values.T
    mean_row = jnp.broadcast_to(mean, (LANES, LANES)).T[0:8]
    hi, mid, low = split3(mean_row)
    row8 = lax.broadcasted_iota(jnp.int32, (8, LANES), 0)
    tail = jnp.where(row8 == 0, hi, jnp.where(row8 == 1, mid, jnp.where(row8 == 2, low, 0.0)))
    tail = to_bf16(jnp.concatenate([tail, jnp.zeros((8, LANES), F32)], axis=0))
    turned = to_bf16(turned)
    slab_t[...] = turned
    for r in range(32):
        pieces[r, 0:32, :] = turned[32 * r : 32 * r + 32]
        pieces[r, 32:48, :] = tail

    lag_rank, space_rank = ranks()
    near = pl.ds(pl.multiple_of(lag_rank // 4 * LANES, LANES), LANES)
    per = jitter.shape[1]
    noise = jnp.concatenate([jitter[0, :, near], jitter[1, :, near], jnp.zeros((96, LANES), F32)], axis=0)
    tmp[...] = noise.T
    noise = tmp[pl.ds(pl.multiple_of(32 * (lag_rank % 4), 32), 32), :]
    lane = lax.broadcasted_iota(jnp.int32, (32, LANES), 1)
    wide[...] = jnp.zeros_like(wide)
    for c in range(CYCLES):
        wide[4 * c : 4 * c + 4, 0:per] = cells[c].astype(F32)
        wide[8 + 4 * c : 12 + 4 * c, 0:per] = weight[c]
        wide[16 + 8 * c : 17 + 8 * c, 0:per] = reading[c : c + 1, :]
    back = lax.rem(LANES - per * space_rank, LANES)
    var = pltpu.roll(jnp.concatenate([variance[...]] * 4, axis=0), back, 1)
    var1 = pltpu.roll(var, per, 1)[1:2]
    var = jnp.where(lane[0:1] < per, var[0:1], jnp.where(lane[0:1] < 2 * per, var1, 0.0))
    read = (wide[16:24, :] + pltpu.roll(wide[24:32, :], per, 1))[0:1]
    error = read + jnp.sqrt(var) * noise
    hi, mid, low = split3(error)
    packed = jnp.where(
        lane < 32,
        hi,
        jnp.where(lane < 64, pltpu.roll(mid, 32, 1), jnp.where(lane < 96, pltpu.roll(low, 64, 1), 0.0)),
    )
    w_hi, w_mid, w_low = split3(wide[8:16, :])
    obs = jnp.concatenate([wide[0:8, :], w_hi, w_mid, w_low], axis=0)
    obs = pltpu.roll(obs, 96, 1)
    packed = jnp.where(lane < 96, packed, jnp.where(lane < 112, obs, 0.0))
    c_hi, c_mid, c_low = split3(coupling[...])
    extra[...] = to_bf16(jnp.concatenate([shift[...].astype(F32), c_hi, c_mid, c_low, packed], axis=0))


def select_kernel(order, arrived, extra, out):
    newest = arrived[order[0]].astype(F32)[0:40]
    piece = to_bf16(jnp.concatenate([newest, extra[...].astype(F32)], axis=0))
    for r in range(out.shape[0]):
        out[r] = piece


def mesh_rows(got, b):
    piece = got[b, 32:64, :].astype(F32)
    lane = lax.broadcasted_iota(jnp.int32, (1, LANES), 1)
    target = lane + piece[8:14].astype(jnp.int32)
    return target, piece[14:20] + piece[20:26] + piece[26:32]


def observation_rows(got, c):
    lane = lax.broadcasted_iota(jnp.int32, (32, LANES), 1)
    error = jnp.zeros((32, LANES), F32)
    obs = jnp.zeros((32, LANES), F32)
    for b in range(got.shape[0]):
        packed = got[b, 64:96, :].astype(F32)
        merged = packed + pltpu.roll(packed, 96, 1) + pltpu.roll(packed, 64, 1)
        mine = (lane >= 16 * b) & (lane < 16 * b + 16)
        error = jnp.where(mine, pltpu.roll(merged, (16 * b - 16 * c) % LANES, 1), error)
        obs = jnp.where(mine, pltpu.roll(packed, (16 * b + 32) % LANES, 1), obs)
    weight = obs[8:16] + obs[16:24] + obs[24:32]
    return error, obs[4 * c : 4 * c + 4].astype(jnp.int32), weight[4 * c : 4 * c + 4]


def build_mesh(got, matrix, total):
    row = lax.broadcasted_iota(jnp.int32, (LANES, LANES), 0)
    low, high = slice(0, 16), slice(LANES - 16, LANES)
    for b in range(got.shape[0]):
        target, weight = mesh_rows(got, b)
        inner = jnp.zeros((LANES, LANES), F32)
        before = jnp.zeros((16, LANES), F32)
        after = jnp.zeros((16, LANES), F32)
        every = jnp.zeros((1, LANES), F32)
        for k in range(6):
            goal = target[k : k + 1]
            at = goal & (LANES - 1)
            here = jnp.where(goal == at, weight[k : k + 1], 0.0)
            there = weight[k : k + 1] - here
            same = row == at
            inner = inner + jnp.where(same, here, 0.0)
            after = after + jnp.where(same[low], there, 0.0)
            before = before + jnp.where(same[high], there, 0.0)
            every = every + weight[k : k + 1]
        total[b] = jnp.broadcast_to(every, (8, LANES))
        edge = jnp.concatenate([after, jnp.zeros((LANES - 32, LANES), F32), before], axis=0)
        for at, part in ((0, inner), (LANES, edge)):
            hi = to_bf16(part)
            matrix[0, b, at : at + LANES, :] = hi
            matrix[1, b, at : at + LANES, :] = to_bf16(part - hi.astype(F32))


def relax(matrix, total, state):
    blocks = state.shape[0]
    lane = lax.broadcasted_iota(jnp.int32, (40, LANES), 1)

    def step(_, carry):
        now = [state[b] for b in range(blocks)]
        zero = jnp.zeros((40, LANES), F32)
        for b in range(blocks):
            before = now[b - 1] if b else zero
            after = now[b + 1] if b + 1 < blocks else zero
            beside = jnp.where(lane < 16, after, jnp.where(lane >= LANES - 16, before, 0.0))
            both = jnp.concatenate([now[b], beside], axis=1)
            hi = both.astype(BF16).astype(F32)
            wide = to_bf16(jnp.concatenate([hi, both - hi], axis=0))
            first = dot(wide, matrix[0, b])
            gain = first[0:40] + (first[40:80] + dot(wide[0:40], matrix[1, b]))
            state[b] = now[b] + (gain - total[b, 0:1, :] * now[b])
        return carry

    lax.fori_loop(0, FC_STEPS, step, 0)


def measure(values, cells, weight):
    lane = lax.broadcasted_iota(jnp.int32, (40, LANES), 1)
    total = jnp.zeros((40, LANES), F32)
    for q in range(4):
        index = jnp.broadcast_to(cells[q : q + 1], (40, LANES))
        picked = jnp.zeros((40, LANES), F32)
        for b, value in enumerate(values):
            mine = (lane >= 16 * b) & (lane < 16 * b + 16)
            picked = jnp.where(mine, jnp.take_along_axis(value, index, axis=1), picked)
        total = total + weight[q : q + 1] * picked
    return total


def observe_kernel(order, one, two, arrived, out, got, state, fields, matrix, total, piece, sems):
    blocks = got.shape[0]
    lags = out.shape[0]
    firsts = (order[lags - 1], order[lags - 2])
    fetch = [
        pltpu.make_async_copy(
            arrived.at[firsts[i], pl.ds(0, 32), :], piece.at[v, pl.ds(64 + 32 * i, 32), :], sems.at[1, 3 * i + v]
        )
        for i in range(2)
        for v in range(3)
        if v != i + 1
    ]
    for copy in fetch:
        copy.start()
    _, space_rank = ranks()
    core = lax.axis_index("core")
    for z in range(one.shape[0]):
        got[2 * z + core] = one[z]
        got[2 * z + 1 - core] = two[z]
    build_mesh(got, matrix, total)
    for b in range(blocks):
        block = got[b, 0:48, :].astype(F32)
        mean = block[32:33] + block[33:34] + block[34:35]
        state[b] = jnp.concatenate([block[0:32], jnp.broadcast_to(mean, (8, LANES))], axis=0)
    relax(matrix, total, state)
    forecast = []
    for b in range(blocks):
        value = state[b]
        rounded = to_bf16(value[0:32])
        fields[b] = rounded
        value = jnp.concatenate([rounded.astype(F32), value[32:40]], axis=0)
        state[b] = value
        forecast.append(value)
    piece[1, 64:96, :] = fields[space_rank]
    error, cells, weight = observation_rows(got, 0)
    seen = measure(forecast, cells, weight)
    spread = seen[0:32] - seen[32:33]
    innovation = error - seen[0:32]
    relax(matrix, total, state)
    piece[2, 96:128, :] = to_bf16(state[space_rank, 0:32, :])
    error, cells, weight = observation_rows(got, 1)
    seen = measure([state[b] for b in range(blocks)], cells, weight)
    spread = to_bf16(jnp.where(core == 0, spread, seen[0:32] - seen[32:33]))
    innovation = to_bf16(jnp.where(core == 0, innovation, error - seen[0:32]))
    for v in range(3):
        piece[v, 0:32, :] = spread
        piece[v, 32:64, :] = innovation
    for copy in fetch:
        copy.wait()
    copies = []
    for r in range(lags):
        pick = jnp.where(firsts[0] == r, 1, jnp.where(firsts[1] == r, 2, 0))
        copies.append(pltpu.make_async_copy(piece.at[pick], out.at[r], sems.at[0, r]))
    for copy in copies:
        copy.start()
    for copy in copies:
        copy.wait()


def run_next(jobs):
    for job in jobs[:2]:
        job()
    del jobs[:2]


def eliminate(d):
    pd = 1.0 / (d[0][0] * d[1][1] - d[0][1] * d[0][1])
    p00, p01, p11 = d[1][1] * pd, -d[0][1] * pd, d[0][0] * pd
    e00 = p00 * d[0][2] + p01 * d[1][2]
    e01 = p00 * d[0][3] + p01 * d[1][3]
    e10 = p01 * d[0][2] + p11 * d[1][2]
    e11 = p01 * d[0][3] + p11 * d[1][3]
    s00 = d[2][2] - (d[0][2] * e00 + d[1][2] * e10)
    s01 = d[2][3] - (d[0][2] * e01 + d[1][2] * e11)
    s11 = d[3][3] - (d[0][3] * e01 + d[1][3] * e11)
    sd = 1.0 / (s00 * s11 - s01 * s01)

    def apply(m):
        y0 = p00 * m[0] + p01 * m[1]
        y1 = p01 * m[0] + p11 * m[1]
        y2 = m[2] - (d[0][2] * y0 + d[1][2] * y1)
        y3 = m[3] - (d[0][3] * y0 + d[1][3] * y1)
        z2 = (s11 * y2 - s01 * y3) * sd
        z3 = (s00 * y3 - s01 * y2) * sd
        return [y0 - (e00 * z2 + e01 * z3), y1 - (e10 * z2 + e11 * z3), z2, z3]

    return apply


def product4(c, z):
    return (c[0] * z[0] + c[1] * z[1]) + (c[2] * z[2] + c[3] * z[3])


def inverse(a, left, right, jobs):
    size = a.shape[0]
    lane = lax.broadcasted_iota(jnp.int32, (8, size), 1)
    tiles = [a[8 * r : 8 * r + 8] for r in range(size // 8)]

    def rows4(tile, o):
        return [jnp.broadcast_to(tile[o + i : o + i + 1, :], (8, size)) for i in range(4)]

    def put(row, k, scaled):
        for i in range(4):
            unit = jnp.where(lane == k + i, 1.0, 0.0)
            left[k + i : k + i + 1, :] = jnp.where(lane < k, row[i], unit)[0:1]
            right[k + i : k + i + 1, :] = jnp.where(lane < k + 4, scaled[i], 0.0)[0:1]

    for t in range(size // 8):
        k = 8 * t
        columns = [
            [jnp.broadcast_to(tiles[r][:, k + j : k + j + 1], (8, size)) for j in range(8)]
            for r in range(t, size // 8)
        ]
        first = (lane >= k) & (lane < k + 4)
        second = (lane >= k + 4) & (lane < k + 8)
        row = rows4(tiles[t], 0)
        d = [rows4(column, 0) for column in columns[0]]
        d = [[d[j][i] for j in range(8)] for i in range(4)]
        apply = eliminate(d)
        scaled = apply([jnp.where(first, jnp.where(lane == k + i, 1.0, 0.0), row[i]) for i in range(4)])
        ahead = [apply([d[i][4 + j] for i in range(4)]) for j in range(4)]
        put(row, k, scaled)
        updated = []
        for r in range(t, size // 8):
            c = columns[r - t]
            tiles[r] = jnp.where(first, 0.0, tiles[r]) - product4(c, scaled)
            updated.append([c[4 + j] - product4(c, ahead[j]) for j in range(4)])
        run_next(jobs)
        row = rows4(tiles[t], 4)
        d = [rows4(column, 4) for column in updated[0]]
        d = [[d[j][i] for j in range(4)] for i in range(4)]
        apply = eliminate(d)
        scaled = apply([jnp.where(second, jnp.where(lane == k + 4 + i, 1.0, 0.0), row[i]) for i in range(4)])
        put(row, k + 4, scaled)
        for r in range(t + 1, size // 8):
            tiles[r] = jnp.where(second, 0.0, tiles[r]) - product4(updated[r - t], scaled)
        run_next(jobs)
    while jobs:
        run_next(jobs)
    return lax.dot_general(
        left[...].T,
        right[...],
        (((1,), (0,)), ((), ())),
        precision=lax.Precision.HIGHEST,
        preferred_element_type=F32,
    )


def dot(a, b):
    return lax.dot_general(a, b, (((1,), (0,)), ((), ())), preferred_element_type=F32)


def centred(values):
    return to_bf16(values - jnp.mean(values, axis=0, keepdims=True))


def stacked(values):
    hi = to_bf16(values)
    return jnp.concatenate([hi, to_bf16(values - hi.astype(F32))], axis=0)


def doubled(values):
    return jnp.concatenate([values, values], axis=1)


def eye():
    rows = lax.broadcasted_iota(jnp.int32, (LANES, LANES), 0)
    return rows == lax.broadcasted_iota(jnp.int32, (LANES, LANES), 1)


def turned(values):
    return values.astype(F32).T.astype(BF16)


def gram_of(spread, spread_t, variance):
    scale = spread_t.shape[0] - 1
    return dot(spread, spread_t) + jnp.where(eye(), scale * variance, 0.0)


def put_gain(gain, i, spread, values):
    gain[i] = stacked(dot(spread, values))


def change(gain, i, rows):
    return dot(rows, gain[i])


def analyse_kernel(
    order, got, other, slab_t, variance, analysed, retired, now, cent, gain, left, right, solved
):
    lags = got.shape[0]
    lag_rank, _ = ranks()
    members = slab_t.shape[0]
    block = members // lags
    mine = pl.ds(pl.multiple_of(lag_rank * block, block), block)
    own_core = lax.axis_index("core")

    def part(i):
        rows = slice(i % 2 * block, (i % 2 + 1) * block)
        values = jnp.where(own_core == i // 2, got[:, rows, :], other[:, rows, :])
        return values.reshape(members, LANES)

    chunks = [slice(LANES * c, LANES * c + LANES) for c in range(members // LANES)]
    holds = (lag_rank == order[lags - 1], lag_rank == order[lags - 2])

    def folded(values):
        return values.reshape(values.shape[0] // 8, 8, LANES).sum(axis=0)

    def centre_jobs(i, load):
        sums = []
        kept = []

        def look(rows):
            def job():
                sums.append(folded(load(rows).astype(F32)))

            return job

        def centre(rows):
            def job():
                if not kept:
                    total = sum(sums[1:], sums[0])
                    kept.append(jnp.sum(total, axis=0, keepdims=True) * (1.0 / members))
                cent[i, rows, :] = to_bf16(now[i, rows, :].astype(F32) - kept[0])

            return job

        return [look(rows) for rows in chunks] + [centre(rows) for rows in chunks]

    def gain_job(i, spread, values):
        return lambda: put_gain(gain, i, spread, values())

    spread = turned(part(0))
    gram = gram_of(spread, part(0), variance[0:1, :])

    def keep(i, load):
        def loaded(rows):
            values = load(rows)
            now[i, rows, :] = values
            return values

        return loaded

    def rows_of(i, rows):
        return got[rows.start // block : rows.stop // block, i * block : (i + 1) * block, :].reshape(LANES, LANES)

    def own_rows(rows):
        return jnp.where(holds[0], rows_of(2, rows), jnp.where(holds[1], rows_of(3, rows), slab_t[rows, :]))

    def retiring(i):
        return lambda rows: jnp.where(holds[i], slab_t[rows, :], rows_of(2 + i, rows))

    jobs = [gain_job(3, spread, lambda: part(2))]
    jobs += centre_jobs(0, keep(0, own_rows))
    jobs += [gain_job(0, spread, lambda: cent[0])]
    jobs += centre_jobs(1, keep(1, retiring(1)))
    jobs += [gain_job(1, spread, lambda: cent[1])]
    jobs += centre_jobs(2, keep(2, retiring(0)))
    jobs += [gain_job(2, spread, lambda: cent[2])]
    solved[...] = doubled(to_bf16(dot(doubled(part(1)), stacked(inverse(gram, left, right, jobs)))))
    seen = change(gain, 3, solved[...])
    spread_t = centred(part(2).astype(F32) + seen)
    innovation = to_bf16(part(3).astype(F32) - seen)
    spread = turned(spread_t)
    gram = gram_of(spread, spread_t, variance[1:2, :])

    def renewed(i):
        def load(rows):
            values = to_bf16(now[i, rows, :].astype(F32) + change(gain, i, solved[rows, :]))
            now[i, rows, :] = values
            return values

        return load

    def retire_first():
        retired[0] = to_bf16(now[2, mine, :].astype(F32) + change(gain, 2, solved[mine, :]))

    jobs = centre_jobs(0, renewed(0)) + centre_jobs(1, renewed(1)) + [retire_first]
    jobs += [gain_job(0, spread, lambda: cent[0]), gain_job(1, spread, lambda: cent[1])]
    solved_again = doubled(to_bf16(dot(doubled(innovation), stacked(inverse(gram, left, right, jobs)))))
    analysed[0] = to_bf16((now[0].astype(F32) + change(gain, 0, solved_again)).T)
    solved[...] = solved_again
    retired[1] = to_bf16(now[1, mine, :].astype(F32) + change(gain, 1, solved[mine, :]))


def stay(values):
    return pltpu.with_memory_space_constraint(values, pltpu.VMEM)


def on_device(
    ensemble,
    slot_order,
    neighbour_shift,
    edge_coupling,
    observation_cells,
    observation_weight,
    observation_reading,
    observation_variance,
    observation_jitter,
):
    lags = lax.axis_size(LAG)
    spaces = lax.axis_size("zh") * lax.axis_size("core")
    per = observation_reading.shape[1]
    members = ensemble.shape[2]

    inputs = (
        ensemble,
        neighbour_shift,
        edge_coupling,
        observation_cells,
        observation_weight,
        observation_reading,
        observation_variance,
        observation_jitter,
    )
    slab_t, pieces, extra = pl.pallas_call(
        prepare_kernel,
        out_shape=[
            jax.ShapeDtypeStruct((members, LANES), BF16),
            jax.ShapeDtypeStruct((lags, FIRST_ROWS, LANES), BF16),
            jax.ShapeDtypeStruct((SECOND_ROWS - 40, LANES), BF16),
        ],
        scratch_shapes=[pltpu.VMEM((LANES, LANES), F32), pltpu.VMEM((32, LANES), F32)],
        name="prepare",
    )(*inputs)

    arrived = lax.all_to_all(pieces, LAG, 0, 0, tiled=True)

    vmem = pl.BlockSpec(memory_space=pltpu.VMEM)
    smem = pl.BlockSpec(memory_space=pltpu.SMEM)
    away = pl.BlockSpec(memory_space=pl.ANY)
    sent = pl.pallas_call(
        select_kernel,
        in_specs=[smem, vmem, vmem],
        out_specs=vmem,
        out_shape=jax.ShapeDtypeStruct((spaces // 2, SECOND_ROWS, LANES), BF16),
        name="select",
    )(slot_order, arrived, extra)
    gathered = lax.all_to_all(sent, "zh", 0, 0, tiled=True)
    swapped = lax.ppermute(gathered, "core", [(0, 1), (1, 0)])
    gathered, swapped = stay(gathered), stay(swapped)

    block = members // lags
    sent = pl.pallas_call(
        observe_kernel,
        in_specs=[smem, vmem, vmem, away],
        out_specs=away,
        out_shape=jax.ShapeDtypeStruct((lags, THIRD * block, LANES), BF16),
        scratch_shapes=[
            pltpu.VMEM((spaces, SECOND_ROWS, LANES), BF16),
            pltpu.VMEM((spaces, 40, LANES), F32),
            pltpu.VMEM((spaces, block, LANES), BF16),
            pltpu.VMEM((2, spaces, 2 * LANES, LANES), BF16),
            pltpu.VMEM((spaces, 8, LANES), F32),
            pltpu.VMEM((3, THIRD * block, LANES), BF16),
            pltpu.SemaphoreType.DMA((2, lags)),
        ],
        name="observe",
    )(slot_order, gathered, swapped, arrived)
    third = lax.all_to_all(sent, LAG, 0, 0, tiled=True)
    other = lax.ppermute(third[:, 0 : 2 * block], "core", [(0, 1), (1, 0)])
    third, other = stay(third), stay(other)

    square = pltpu.VMEM((LANES, LANES), F32)
    return pl.pallas_call(
        analyse_kernel,
        in_specs=[smem, vmem, vmem, vmem, vmem],
        out_specs=[vmem, vmem],
        out_shape=[
            jax.ShapeDtypeStruct(ensemble.shape, BF16),
            jax.ShapeDtypeStruct((CYCLES, block, LANES), BF16),
        ],
        scratch_shapes=[
            pltpu.VMEM((3, members, LANES), BF16),
            pltpu.VMEM((3, members, LANES), BF16),
            pltpu.VMEM((4, 2 * LANES, LANES), BF16),
            square,
            square,
            pltpu.VMEM((members, 2 * LANES), BF16),
        ],
        name="analyse",
    )(slot_order, third, other, slab_t, observation_variance)


def solution(mesh):
    split = Mesh(
        mesh.devices.reshape(4, 2, 4, mesh.shape["space"] // 2, 2), LAG + ("zh", "core")
    )
    space = ("zh", "core")
    placed = (
        P(LAG, space, None),
        P(),
        P(None, space),
        P(None, space),
        P(None, None, space),
        P(None, None, space),
        P(None, space),
        P(),
        P(None, space, None),
    )
    return jax.shard_map(
        on_device,
        mesh=split,
        in_specs=placed,
        out_specs=(P(LAG, space, None), P(None, LAG, space)),
        check_vma=False,
    )
```

```python
import jax
import jax.numpy as jnp
from jax import lax
from jax.experimental import pallas as pl
from jax.experimental.pallas import tpu as pltpu
from jax.sharding import Mesh
from jax.sharding import PartitionSpec as P

FC_STEPS = 4
CYCLES = 2
LAG = ("lag_0", "lag_1", "lag_2")
F32 = jnp.float32
BF16 = jnp.bfloat16
LANES = 128
FIRST_ROWS = 48
SECOND_ROWS = 96
THIRD = 4


def split3(x):
    hi = x.astype(BF16).astype(F32)
    mid = (x - hi).astype(BF16).astype(F32)
    low = (x - hi - mid).astype(BF16).astype(F32)
    return hi, mid, low


def to_bf16(x):
    return x.astype(BF16)


def ranks():
    return lax.axis_index(LAG), lax.axis_index("zh") * lax.axis_size("core") + lax.axis_index("core")


def prepare_kernel(
    slab, shift, coupling, cells, weight, reading, variance, jitter, slab_t, pieces, extra, tmp, wide
):
    values = slab[0].astype(F32)
    mean = jnp.mean(values, axis=1, keepdims=True)
    mean_row = jnp.broadcast_to(mean, (LANES, LANES)).T[0:8]
    hi, mid, low = split3(mean_row)
    row8 = lax.broadcasted_iota(jnp.int32, (8, LANES), 0)
    tail = jnp.where(row8 == 0, hi, jnp.where(row8 == 1, mid, jnp.where(row8 == 2, low, 0.0)))
    tail = to_bf16(jnp.concatenate([tail, jnp.zeros((8, LANES), F32)], axis=0))
    turned = slab[0].T
    slab_t[...] = turned
    for r in range(32):
        pieces[r, 0:32, :] = turned[32 * r : 32 * r + 32]
        pieces[r, 32:48, :] = tail

    lag_rank, space_rank = ranks()
    near = pl.ds(pl.multiple_of(lag_rank // 4 * LANES, LANES), LANES)
    per = jitter.shape[1]
    noise = jnp.concatenate([jitter[0, :, near], jitter[1, :, near], jnp.zeros((96, LANES), F32)], axis=0)
    tmp[...] = noise.T
    noise = tmp[pl.ds(pl.multiple_of(32 * (lag_rank % 4), 32), 32), :]
    lane = lax.broadcasted_iota(jnp.int32, (32, LANES), 1)
    wide[...] = jnp.zeros_like(wide)
    for c in range(CYCLES):
        wide[4 * c : 4 * c + 4, 0:per] = cells[c].astype(F32)
        wide[8 + 4 * c : 12 + 4 * c, 0:per] = weight[c]
        wide[16 + 8 * c : 17 + 8 * c, 0:per] = reading[c : c + 1, :]
    back = lax.rem(LANES - per * space_rank, LANES)
    var = pltpu.roll(jnp.concatenate([variance[...]] * 4, axis=0), back, 1)
    var1 = pltpu.roll(var, per, 1)[1:2]
    var = jnp.where(lane[0:1] < per, var[0:1], jnp.where(lane[0:1] < 2 * per, var1, 0.0))
    read = (wide[16:24, :] + pltpu.roll(wide[24:32, :], per, 1))[0:1]
    error = read + jnp.sqrt(var) * noise
    hi, mid, low = split3(error)
    packed = jnp.where(
        lane < 32,
        hi,
        jnp.where(lane < 64, pltpu.roll(mid, 32, 1), jnp.where(lane < 96, pltpu.roll(low, 64, 1), 0.0)),
    )
    w_hi, w_mid, w_low = split3(wide[8:16, :])
    obs = jnp.concatenate([wide[0:8, :], w_hi, w_mid, w_low], axis=0)
    obs = pltpu.roll(obs, 96, 1)
    packed = jnp.where(lane < 96, packed, jnp.where(lane < 112, obs, 0.0))
    c_hi, c_mid, c_low = split3(coupling[...])
    extra[...] = to_bf16(jnp.concatenate([shift[...].astype(F32), c_hi, c_mid, c_low, packed], axis=0))


def select_kernel(order, arrived, extra, out):
    newest = arrived[order[0]].astype(F32)[0:40]
    piece = to_bf16(jnp.concatenate([newest, extra[...].astype(F32)], axis=0))
    for r in range(out.shape[0]):
        out[r] = piece


def mesh_rows(got, b):
    piece = got[b, 32:64, :].astype(F32)
    lane = lax.broadcasted_iota(jnp.int32, (1, LANES), 1)
    target = lane + piece[8:14].astype(jnp.int32)
    return target, piece[14:20] + piece[20:26] + piece[26:32]


def observation_rows(got, c):
    lane = lax.broadcasted_iota(jnp.int32, (32, LANES), 1)
    error = jnp.zeros((32, LANES), F32)
    obs = jnp.zeros((32, LANES), F32)
    for b in range(got.shape[0]):
        packed = got[b, 64:96, :].astype(F32)
        merged = packed + pltpu.roll(packed, 96, 1) + pltpu.roll(packed, 64, 1)
        mine = (lane >= 16 * b) & (lane < 16 * b + 16)
        error = jnp.where(mine, pltpu.roll(merged, (16 * b - 16 * c) % LANES, 1), error)
        obs = jnp.where(mine, pltpu.roll(packed, (16 * b + 32) % LANES, 1), obs)
    weight = obs[8:16] + obs[16:24] + obs[24:32]
    return error, obs[4 * c : 4 * c + 4].astype(jnp.int32), weight[4 * c : 4 * c + 4]


def build_mesh(got, matrix, total):
    row = lax.broadcasted_iota(jnp.int32, (LANES, LANES), 0)
    low, high = slice(0, 16), slice(LANES - 16, LANES)
    for b in range(got.shape[0]):
        target, weight = mesh_rows(got, b)
        inner = jnp.zeros((LANES, LANES), F32)
        before = jnp.zeros((16, LANES), F32)
        after = jnp.zeros((16, LANES), F32)
        every = jnp.zeros((1, LANES), F32)
        for k in range(6):
            goal = target[k : k + 1]
            at = goal & (LANES - 1)
            here = jnp.where(goal == at, weight[k : k + 1], 0.0)
            there = weight[k : k + 1] - here
            same = row == at
            inner = inner + jnp.where(same, here, 0.0)
            after = after + jnp.where(same[low], there, 0.0)
            before = before + jnp.where(same[high], there, 0.0)
            every = every + weight[k : k + 1]
        total[b] = jnp.broadcast_to(every, (8, LANES))
        edge = jnp.concatenate([after, jnp.zeros((LANES - 32, LANES), F32), before], axis=0)
        for at, part in ((0, inner), (LANES, edge)):
            hi = to_bf16(part)
            matrix[0, b, at : at + LANES, :] = hi
            matrix[1, b, at : at + LANES, :] = to_bf16(part - hi.astype(F32))


def relax(matrix, total, state):
    blocks = state.shape[0]
    lane = lax.broadcasted_iota(jnp.int32, (40, LANES), 1)

    def step(_, carry):
        now = [state[b] for b in range(blocks)]
        zero = jnp.zeros((40, LANES), F32)
        for b in range(blocks):
            before = now[b - 1] if b else zero
            after = now[b + 1] if b + 1 < blocks else zero
            beside = jnp.where(lane < 16, after, jnp.where(lane >= LANES - 16, before, 0.0))
            both = jnp.concatenate([now[b], beside], axis=1)
            hi = both.astype(BF16).astype(F32)
            wide = to_bf16(jnp.concatenate([hi, both - hi], axis=0))
            first = dot(wide, matrix[0, b])
            gain = first[0:40] + (first[40:80] + dot(wide[0:40], matrix[1, b]))
            state[b] = now[b] + (gain - total[b, 0:1, :] * now[b])
        return carry

    lax.fori_loop(0, FC_STEPS, step, 0)


def measure(values, cells, weight):
    lane = lax.broadcasted_iota(jnp.int32, (40, LANES), 1)
    total = jnp.zeros((40, LANES), F32)
    for q in range(4):
        index = jnp.broadcast_to(cells[q : q + 1], (40, LANES))
        picked = jnp.zeros((40, LANES), F32)
        for b, value in enumerate(values):
            mine = (lane >= 16 * b) & (lane < 16 * b + 16)
            picked = jnp.where(mine, jnp.take_along_axis(value, index, axis=1), picked)
        total = total + weight[q : q + 1] * picked
    return total


def observe_kernel(order, one, two, arrived, out, got, state, fields, matrix, total, piece, sems):
    blocks = got.shape[0]
    lags = out.shape[0]
    firsts = (order[lags - 1], order[lags - 2])
    for i in range(2):
        slab = arrived[firsts[i], 0:32, :]
        for v in range(3):
            if v != i + 1:
                piece[v, 64 + 32 * i : 96 + 32 * i, :] = slab
    _, space_rank = ranks()
    core = lax.axis_index("core")
    for z in range(one.shape[0]):
        got[2 * z + core] = one[z]
        got[2 * z + 1 - core] = two[z]
    build_mesh(got, matrix, total)
    for b in range(blocks):
        block = got[b, 0:48, :].astype(F32)
        mean = block[32:33] + block[33:34] + block[34:35]
        state[b] = jnp.concatenate([block[0:32], jnp.broadcast_to(mean, (8, LANES))], axis=0)
    relax(matrix, total, state)
    forecast = []
    for b in range(blocks):
        value = state[b]
        rounded = to_bf16(value[0:32])
        fields[b] = rounded
        value = jnp.concatenate([rounded.astype(F32), value[32:40]], axis=0)
        state[b] = value
        forecast.append(value)
    piece[1, 64:96, :] = fields[space_rank]
    error, cells, weight = observation_rows(got, 0)
    seen = measure(forecast, cells, weight)
    spread = seen[0:32] - seen[32:33]
    innovation = error - seen[0:32]
    relax(matrix, total, state)
    piece[2, 96:128, :] = to_bf16(state[space_rank, 0:32, :])
    error, cells, weight = observation_rows(got, 1)
    seen = measure([state[b] for b in range(blocks)], cells, weight)
    spread = to_bf16(jnp.where(core == 0, spread, seen[0:32] - seen[32:33]))
    innovation = to_bf16(jnp.where(core == 0, innovation, error - seen[0:32]))
    for v in range(3):
        piece[v, 0:32, :] = spread
        piece[v, 32:64, :] = innovation
    copies = []
    for r in range(lags):
        pick = jnp.where(firsts[0] == r, 1, jnp.where(firsts[1] == r, 2, 0))
        copies.append(pltpu.make_async_copy(piece.at[pick], out.at[r], sems.at[r]))
    for copy in copies:
        copy.start()
    for copy in copies:
        copy.wait()


def run_next(jobs):
    for job in jobs[:2]:
        job()
    del jobs[:2]


def eliminate(d):
    pd = 1.0 / (d[0][0] * d[1][1] - d[0][1] * d[0][1])
    p00, p01, p11 = d[1][1] * pd, -d[0][1] * pd, d[0][0] * pd
    e00 = p00 * d[0][2] + p01 * d[1][2]
    e01 = p00 * d[0][3] + p01 * d[1][3]
    e10 = p01 * d[0][2] + p11 * d[1][2]
    e11 = p01 * d[0][3] + p11 * d[1][3]
    s00 = d[2][2] - (d[0][2] * e00 + d[1][2] * e10)
    s01 = d[2][3] - (d[0][2] * e01 + d[1][2] * e11)
    s11 = d[3][3] - (d[0][3] * e01 + d[1][3] * e11)
    sd = 1.0 / (s00 * s11 - s01 * s01)

    def apply(m):
        y0 = p00 * m[0] + p01 * m[1]
        y1 = p01 * m[0] + p11 * m[1]
        y2 = m[2] - (d[0][2] * y0 + d[1][2] * y1)
        y3 = m[3] - (d[0][3] * y0 + d[1][3] * y1)
        z2 = (s11 * y2 - s01 * y3) * sd
        z3 = (s00 * y3 - s01 * y2) * sd
        return [y0 - (e00 * z2 + e01 * z3), y1 - (e10 * z2 + e11 * z3), z2, z3]

    return apply


def product4(c, z):
    return (c[0] * z[0] + c[1] * z[1]) + (c[2] * z[2] + c[3] * z[3])


def inverse(a, left, right, jobs):
    size = a.shape[0]
    lane = lax.broadcasted_iota(jnp.int32, (8, size), 1)
    tiles = [a[8 * r : 8 * r + 8] for r in range(size // 8)]

    def rows4(tile, o):
        return [jnp.broadcast_to(tile[o + i : o + i + 1, :], (8, size)) for i in range(4)]

    def put(row, k, scaled):
        for i in range(4):
            unit = jnp.where(lane == k + i, 1.0, 0.0)
            left[k + i : k + i + 1, :] = jnp.where(lane < k, row[i], unit)[0:1]
            right[k + i : k + i + 1, :] = jnp.where(lane < k + 4, scaled[i], 0.0)[0:1]

    for t in range(size // 8):
        k = 8 * t
        columns = [
            [jnp.broadcast_to(tiles[r][:, k + j : k + j + 1], (8, size)) for j in range(8)]
            for r in range(t, size // 8)
        ]
        first = (lane >= k) & (lane < k + 4)
        second = (lane >= k + 4) & (lane < k + 8)
        row = rows4(tiles[t], 0)
        d = [rows4(column, 0) for column in columns[0]]
        d = [[d[j][i] for j in range(8)] for i in range(4)]
        apply = eliminate(d)
        scaled = apply([jnp.where(first, jnp.where(lane == k + i, 1.0, 0.0), row[i]) for i in range(4)])
        ahead = [apply([d[i][4 + j] for i in range(4)]) for j in range(4)]
        put(row, k, scaled)
        updated = []
        for r in range(t, size // 8):
            c = columns[r - t]
            tiles[r] = jnp.where(first, 0.0, tiles[r]) - product4(c, scaled)
            updated.append([c[4 + j] - product4(c, ahead[j]) for j in range(4)])
        run_next(jobs)
        row = rows4(tiles[t], 4)
        d = [rows4(column, 4) for column in updated[0]]
        d = [[d[j][i] for j in range(4)] for i in range(4)]
        apply = eliminate(d)
        scaled = apply([jnp.where(second, jnp.where(lane == k + 4 + i, 1.0, 0.0), row[i]) for i in range(4)])
        put(row, k + 4, scaled)
        for r in range(t + 1, size // 8):
            tiles[r] = jnp.where(second, 0.0, tiles[r]) - product4(updated[r - t], scaled)
        run_next(jobs)
    while jobs:
        run_next(jobs)
    return lax.dot_general(
        left[...].T,
        right[...],
        (((1,), (0,)), ((), ())),
        precision=lax.Precision.HIGHEST,
        preferred_element_type=F32,
    )


def dot(a, b):
    return lax.dot_general(a, b, (((1,), (0,)), ((), ())), preferred_element_type=F32)


def centred(values):
    return to_bf16(values - jnp.mean(values, axis=0, keepdims=True))


def stacked(values):
    hi = to_bf16(values)
    return jnp.concatenate([hi, to_bf16(values - hi.astype(F32))], axis=0)


def doubled(values):
    return jnp.concatenate([values, values], axis=1)


def eye():
    rows = lax.broadcasted_iota(jnp.int32, (LANES, LANES), 0)
    return rows == lax.broadcasted_iota(jnp.int32, (LANES, LANES), 1)


def turned(values):
    return values.T


def gram_of(spread, spread_t, variance):
    scale = spread_t.shape[0] - 1
    return dot(spread, spread_t) + jnp.where(eye(), scale * variance, 0.0)


def put_gain(gain, i, spread, values):
    gain[i] = stacked(dot(spread, values))


def change(gain, i, rows):
    return dot(rows, gain[i])


def analyse_kernel(
    order, got, other, slab_t, variance, analysed, retired, now, cent, gain, left, right, solved
):
    lags = got.shape[0]
    lag_rank, _ = ranks()
    members = slab_t.shape[0]
    block = members // lags
    mine = pl.ds(pl.multiple_of(lag_rank * block, block), block)
    own_core = lax.axis_index("core")

    def part(i):
        rows = slice(i % 2 * block, (i % 2 + 1) * block)
        values = jnp.where(own_core == i // 2, got[:, rows, :], other[:, rows, :])
        return values.reshape(members, LANES)

    chunks = [slice(LANES * c, LANES * c + LANES) for c in range(members // LANES)]
    holds = (lag_rank == order[lags - 1], lag_rank == order[lags - 2])

    def folded(values):
        return values.reshape(values.shape[0] // 8, 8, LANES).sum(axis=0)

    def centre_jobs(i, load):
        sums = []
        kept = []

        def look(rows):
            def job():
                sums.append(folded(load(rows).astype(F32)))

            return job

        def centre(rows):
            def job():
                if not kept:
                    total = sum(sums[1:], sums[0])
                    kept.append(jnp.sum(total, axis=0, keepdims=True) * (1.0 / members))
                cent[i, rows, :] = to_bf16(now[i, rows, :].astype(F32) - kept[0])

            return job

        return [look(rows) for rows in chunks] + [centre(rows) for rows in chunks]

    def gain_job(i, spread, values):
        return lambda: put_gain(gain, i, spread, values())

    spread = turned(part(0))
    gram = gram_of(spread, part(0), variance[0:1, :])

    def keep(i, load):
        def loaded(rows):
            values = load(rows)
            now[i, rows, :] = values
            return values

        return loaded

    def rows_of(i, rows):
        return got[rows.start // block : rows.stop // block, i * block : (i + 1) * block, :].reshape(LANES, LANES)

    def own_rows(rows):
        return jnp.where(holds[0], rows_of(2, rows), jnp.where(holds[1], rows_of(3, rows), slab_t[rows, :]))

    def retiring(i):
        return lambda rows: jnp.where(holds[i], slab_t[rows, :], rows_of(2 + i, rows))

    jobs = [gain_job(3, spread, lambda: part(2))]
    jobs += centre_jobs(0, keep(0, own_rows))
    jobs += [gain_job(0, spread, lambda: cent[0])]
    jobs += centre_jobs(1, keep(1, retiring(1)))
    jobs += [gain_job(1, spread, lambda: cent[1])]
    jobs += centre_jobs(2, keep(2, retiring(0)))
    jobs += [gain_job(2, spread, lambda: cent[2])]
    solved[...] = doubled(to_bf16(dot(doubled(part(1)), stacked(inverse(gram, left, right, jobs)))))
    seen = change(gain, 3, solved[...])
    spread_t = centred(part(2).astype(F32) + seen)
    innovation = to_bf16(part(3).astype(F32) - seen)
    spread = turned(spread_t)
    gram = gram_of(spread, spread_t, variance[1:2, :])

    def renewed(i):
        def load(rows):
            values = to_bf16(now[i, rows, :].astype(F32) + change(gain, i, solved[rows, :]))
            now[i, rows, :] = values
            return values

        return load

    def retire_first():
        retired[0] = to_bf16(now[2, mine, :].astype(F32) + change(gain, 2, solved[mine, :]))

    jobs = centre_jobs(0, renewed(0)) + centre_jobs(1, renewed(1)) + [retire_first]
    jobs += [gain_job(0, spread, lambda: cent[0]), gain_job(1, spread, lambda: cent[1])]
    solved_again = doubled(to_bf16(dot(doubled(innovation), stacked(inverse(gram, left, right, jobs)))))
    analysed[0] = to_bf16(now[0].astype(F32) + change(gain, 0, solved_again)).T
    solved[...] = solved_again
    retired[1] = to_bf16(now[1, mine, :].astype(F32) + change(gain, 1, solved[mine, :]))


def stay(values):
    return pltpu.with_memory_space_constraint(values, pltpu.VMEM)


def on_device(
    ensemble,
    slot_order,
    neighbour_shift,
    edge_coupling,
    observation_cells,
    observation_weight,
    observation_reading,
    observation_variance,
    observation_jitter,
):
    lags = lax.axis_size(LAG)
    spaces = lax.axis_size("zh") * lax.axis_size("core")
    per = observation_reading.shape[1]
    members = ensemble.shape[2]

    inputs = (
        ensemble,
        neighbour_shift,
        edge_coupling,
        observation_cells,
        observation_weight,
        observation_reading,
        observation_variance,
        observation_jitter,
    )
    slab_t, pieces, extra = pl.pallas_call(
        prepare_kernel,
        out_shape=[
            jax.ShapeDtypeStruct((members, LANES), BF16),
            jax.ShapeDtypeStruct((lags, FIRST_ROWS, LANES), BF16),
            jax.ShapeDtypeStruct((SECOND_ROWS - 40, LANES), BF16),
        ],
        scratch_shapes=[pltpu.VMEM((LANES, LANES), F32), pltpu.VMEM((32, LANES), F32)],
        name="prepare",
    )(*inputs)

    arrived = stay(lax.all_to_all(pieces, LAG, 0, 0, tiled=True))
    slab_t, extra = stay(slab_t), stay(extra)

    vmem = pl.BlockSpec(memory_space=pltpu.VMEM)
    smem = pl.BlockSpec(memory_space=pltpu.SMEM)
    away = pl.BlockSpec(memory_space=pl.ANY)
    sent = pl.pallas_call(
        select_kernel,
        in_specs=[smem, vmem, vmem],
        out_specs=vmem,
        out_shape=jax.ShapeDtypeStruct((spaces // 2, SECOND_ROWS, LANES), BF16),
        name="select",
    )(slot_order, arrived, extra)
    gathered = lax.all_to_all(sent, "zh", 0, 0, tiled=True)
    swapped = lax.ppermute(gathered, "core", [(0, 1), (1, 0)])
    gathered, swapped = stay(gathered), stay(swapped)

    block = members // lags
    sent = pl.pallas_call(
        observe_kernel,
        in_specs=[smem, vmem, vmem, vmem],
        out_specs=away,
        out_shape=jax.ShapeDtypeStruct((lags, THIRD * block, LANES), BF16),
        scratch_shapes=[
            pltpu.VMEM((spaces, SECOND_ROWS, LANES), BF16),
            pltpu.VMEM((spaces, 40, LANES), F32),
            pltpu.VMEM((spaces, block, LANES), BF16),
            pltpu.VMEM((2, spaces, 2 * LANES, LANES), BF16),
            pltpu.VMEM((spaces, 8, LANES), F32),
            pltpu.VMEM((3, THIRD * block, LANES), BF16),
            pltpu.SemaphoreType.DMA((lags,)),
        ],
        name="observe",
    )(slot_order, gathered, swapped, arrived)
    third = lax.all_to_all(sent, LAG, 0, 0, tiled=True)
    other = lax.ppermute(third[:, 0 : 2 * block], "core", [(0, 1), (1, 0)])
    third, other = stay(third), stay(other)

    square = pltpu.VMEM((LANES, LANES), F32)
    return pl.pallas_call(
        analyse_kernel,
        in_specs=[smem, vmem, vmem, vmem, vmem],
        out_specs=[vmem, vmem],
        out_shape=[
            jax.ShapeDtypeStruct(ensemble.shape, BF16),
            jax.ShapeDtypeStruct((CYCLES, block, LANES), BF16),
        ],
        scratch_shapes=[
            pltpu.VMEM((3, members, LANES), BF16),
            pltpu.VMEM((3, members, LANES), BF16),
            pltpu.VMEM((4, 2 * LANES, LANES), BF16),
            square,
            square,
            pltpu.VMEM((members, 2 * LANES), BF16),
        ],
        name="analyse",
    )(slot_order, third, other, slab_t, observation_variance)


def solution(mesh):
    split = Mesh(
        mesh.devices.reshape(4, 2, 4, mesh.shape["space"] // 2, 2), LAG + ("zh", "core")
    )
    space = ("zh", "core")
    placed = (
        P(LAG, space, None),
        P(),
        P(None, space),
        P(None, space),
        P(None, None, space),
        P(None, None, space),
        P(None, space),
        P(),
        P(None, space, None),
    )
    return jax.shard_map(
        on_device,
        mesh=split,
        in_specs=placed,
        out_specs=(P(LAG, space, None), P(None, LAG, space)),
        check_vma=False,
    )
```

```python
import jax
import jax.numpy as jnp
from jax import lax
from jax.experimental import pallas as pl
from jax.experimental.pallas import tpu as pltpu
from jax.sharding import Mesh
from jax.sharding import PartitionSpec as P

FC_STEPS = 4
CYCLES = 2
LAG = ("lag_0", "lag_1", "lag_2")
F32 = jnp.float32
BF16 = jnp.bfloat16
LANES = 128
FIRST_ROWS = 48
SECOND_ROWS = 96
THIRD = 4


def split3(x):
    hi = x.astype(BF16).astype(F32)
    mid = (x - hi).astype(BF16).astype(F32)
    low = (x - hi - mid).astype(BF16).astype(F32)
    return hi, mid, low


def to_bf16(x):
    return x.astype(BF16)


def ranks():
    return lax.axis_index(LAG), lax.axis_index("zh") * lax.axis_size("core") + lax.axis_index("core")


def prepare_kernel(
    slab, shift, coupling, cells, weight, reading, variance, jitter, slab_t, pieces, extra, tmp, wide
):
    values = slab[0].astype(F32)
    mean = jnp.mean(values, axis=1, keepdims=True)
    mean_row = jnp.broadcast_to(mean, (LANES, LANES)).T[0:8]
    hi, mid, low = split3(mean_row)
    row8 = lax.broadcasted_iota(jnp.int32, (8, LANES), 0)
    tail = jnp.where(row8 == 0, hi, jnp.where(row8 == 1, mid, jnp.where(row8 == 2, low, 0.0)))
    tail = to_bf16(jnp.concatenate([tail, jnp.zeros((8, LANES), F32)], axis=0))
    turned = slab[0].T
    slab_t[...] = turned
    for r in range(32):
        pieces[r, 0:32, :] = turned[32 * r : 32 * r + 32]
        pieces[r, 32:48, :] = tail

    lag_rank, space_rank = ranks()
    near = pl.ds(pl.multiple_of(lag_rank // 4 * LANES, LANES), LANES)
    per = jitter.shape[1]
    noise = jnp.concatenate([jitter[0, :, near], jitter[1, :, near], jnp.zeros((96, LANES), F32)], axis=0)
    tmp[...] = noise.T
    noise = tmp[pl.ds(pl.multiple_of(32 * (lag_rank % 4), 32), 32), :]
    lane = lax.broadcasted_iota(jnp.int32, (32, LANES), 1)
    wide[...] = jnp.zeros_like(wide)
    for c in range(CYCLES):
        wide[4 * c : 4 * c + 4, 0:per] = cells[c].astype(F32)
        wide[8 + 4 * c : 12 + 4 * c, 0:per] = weight[c]
        wide[16 + 8 * c : 17 + 8 * c, 0:per] = reading[c : c + 1, :]
    back = lax.rem(LANES - per * space_rank, LANES)
    var = pltpu.roll(jnp.concatenate([variance[...]] * 4, axis=0), back, 1)
    var1 = pltpu.roll(var, per, 1)[1:2]
    var = jnp.where(lane[0:1] < per, var[0:1], jnp.where(lane[0:1] < 2 * per, var1, 0.0))
    read = (wide[16:24, :] + pltpu.roll(wide[24:32, :], per, 1))[0:1]
    error = read + jnp.sqrt(var) * noise
    hi, mid, low = split3(error)
    packed = jnp.where(
        lane < 32,
        hi,
        jnp.where(lane < 64, pltpu.roll(mid, 32, 1), jnp.where(lane < 96, pltpu.roll(low, 64, 1), 0.0)),
    )
    w_hi, w_mid, w_low = split3(wide[8:16, :])
    obs = jnp.concatenate([wide[0:8, :], w_hi, w_mid, w_low], axis=0)
    obs = pltpu.roll(obs, 96, 1)
    packed = jnp.where(lane < 96, packed, jnp.where(lane < 112, obs, 0.0))
    c_hi, c_mid, c_low = split3(coupling[...])
    extra[...] = to_bf16(jnp.concatenate([shift[...].astype(F32), c_hi, c_mid, c_low, packed], axis=0))


def select_kernel(order, arrived, extra, out):
    newest = arrived[order[0]].astype(F32)[0:40]
    piece = to_bf16(jnp.concatenate([newest, extra[...].astype(F32)], axis=0))
    for r in range(out.shape[0]):
        out[r] = piece


def mesh_rows(got, b):
    piece = got[b, 32:64, :].astype(F32)
    lane = lax.broadcasted_iota(jnp.int32, (1, LANES), 1)
    target = lane + piece[8:14].astype(jnp.int32)
    return target, piece[14:20] + piece[20:26] + piece[26:32]


def observation_rows(got, c):
    lane = lax.broadcasted_iota(jnp.int32, (32, LANES), 1)
    error = jnp.zeros((32, LANES), F32)
    obs = jnp.zeros((32, LANES), F32)
    for b in range(got.shape[0]):
        packed = got[b, 64:96, :].astype(F32)
        merged = packed + pltpu.roll(packed, 96, 1) + pltpu.roll(packed, 64, 1)
        mine = (lane >= 16 * b) & (lane < 16 * b + 16)
        error = jnp.where(mine, pltpu.roll(merged, (16 * b - 16 * c) % LANES, 1), error)
        obs = jnp.where(mine, pltpu.roll(packed, (16 * b + 32) % LANES, 1), obs)
    weight = obs[8:16] + obs[16:24] + obs[24:32]
    return error, obs[4 * c : 4 * c + 4].astype(jnp.int32), weight[4 * c : 4 * c + 4]


def build_mesh(got, matrix, total):
    row = lax.broadcasted_iota(jnp.int32, (LANES, LANES), 0)
    low, high = slice(0, 16), slice(LANES - 16, LANES)
    for b in range(got.shape[0]):
        target, weight = mesh_rows(got, b)
        inner = jnp.zeros((LANES, LANES), F32)
        before = jnp.zeros((16, LANES), F32)
        after = jnp.zeros((16, LANES), F32)
        every = jnp.zeros((1, LANES), F32)
        for k in range(6):
            goal = target[k : k + 1]
            at = goal & (LANES - 1)
            here = jnp.where(goal == at, weight[k : k + 1], 0.0)
            there = weight[k : k + 1] - here
            same = row == at
            inner = inner + jnp.where(same, here, 0.0)
            after = after + jnp.where(same[low], there, 0.0)
            before = before + jnp.where(same[high], there, 0.0)
            every = every + weight[k : k + 1]
        total[b] = jnp.broadcast_to(every, (8, LANES))
        edge = jnp.concatenate([after, jnp.zeros((LANES - 32, LANES), F32), before], axis=0)
        for at, part in ((0, inner), (LANES, edge)):
            hi = to_bf16(part)
            matrix[0, b, at : at + LANES, :] = hi
            matrix[1, b, at : at + LANES, :] = to_bf16(part - hi.astype(F32))


def relax(matrix, total, state):
    blocks = state.shape[0]
    lane = lax.broadcasted_iota(jnp.int32, (40, LANES), 1)

    zero = jnp.zeros((40, LANES), F32)
    now = [state[b] for b in range(blocks)]
    for _ in range(FC_STEPS):
        after_step = []
        for b in range(blocks):
            before = now[b - 1] if b else zero
            after = now[b + 1] if b + 1 < blocks else zero
            beside = jnp.where(lane < 16, after, jnp.where(lane >= LANES - 16, before, 0.0))
            both = jnp.concatenate([now[b], beside], axis=1)
            hi = both.astype(BF16).astype(F32)
            wide = to_bf16(jnp.concatenate([hi, both - hi], axis=0))
            first = dot(wide, matrix[0, b])
            gain = first[0:40] + (first[40:80] + dot(wide[0:40], matrix[1, b]))
            after_step.append(now[b] + (gain - total[b, 0:1, :] * now[b]))
        now = after_step
    for b in range(blocks):
        state[b] = now[b]


def measure(values, cells, weight):
    lane = lax.broadcasted_iota(jnp.int32, (40, LANES), 1)
    total = jnp.zeros((40, LANES), F32)
    for q in range(4):
        index = jnp.broadcast_to(cells[q : q + 1], (40, LANES))
        picked = jnp.zeros((40, LANES), F32)
        for b, value in enumerate(values):
            mine = (lane >= 16 * b) & (lane < 16 * b + 16)
            picked = jnp.where(mine, jnp.take_along_axis(value, index, axis=1), picked)
        total = total + weight[q : q + 1] * picked
    return total


def observe_kernel(order, one, two, arrived, out, got, state, fields, matrix, total, piece, sems):
    blocks = got.shape[0]
    lags = out.shape[0]
    firsts = (order[lags - 1], order[lags - 2])
    for i in range(2):
        slab = arrived[firsts[i], 0:32, :]
        for v in range(3):
            if v != i + 1:
                piece[v, 64 + 32 * i : 96 + 32 * i, :] = slab
    _, space_rank = ranks()
    core = lax.axis_index("core")
    for z in range(one.shape[0]):
        got[2 * z + core] = one[z]
        got[2 * z + 1 - core] = two[z]
    build_mesh(got, matrix, total)
    for b in range(blocks):
        block = got[b, 0:48, :].astype(F32)
        mean = block[32:33] + block[33:34] + block[34:35]
        state[b] = jnp.concatenate([block[0:32], jnp.broadcast_to(mean, (8, LANES))], axis=0)
    relax(matrix, total, state)
    forecast = []
    for b in range(blocks):
        value = state[b]
        rounded = to_bf16(value[0:32])
        fields[b] = rounded
        value = jnp.concatenate([rounded.astype(F32), value[32:40]], axis=0)
        state[b] = value
        forecast.append(value)
    piece[1, 64:96, :] = fields[space_rank]
    error, cells, weight = observation_rows(got, 0)
    seen = measure(forecast, cells, weight)
    spread = seen[0:32] - seen[32:33]
    innovation = error - seen[0:32]
    relax(matrix, total, state)
    piece[2, 96:128, :] = to_bf16(state[space_rank, 0:32, :])
    error, cells, weight = observation_rows(got, 1)
    seen = measure([state[b] for b in range(blocks)], cells, weight)
    spread = to_bf16(jnp.where(core == 0, spread, seen[0:32] - seen[32:33]))
    innovation = to_bf16(jnp.where(core == 0, innovation, error - seen[0:32]))
    for v in range(3):
        piece[v, 0:32, :] = spread
        piece[v, 32:64, :] = innovation
    copies = []
    for r in range(lags):
        pick = jnp.where(firsts[0] == r, 1, jnp.where(firsts[1] == r, 2, 0))
        copies.append(pltpu.make_async_copy(piece.at[pick], out.at[r], sems.at[r]))
    for copy in copies:
        copy.start()
    for copy in copies:
        copy.wait()


def run_next(jobs):
    for job in jobs[:2]:
        job()
    del jobs[:2]


def eliminate(d):
    pd = 1.0 / (d[0][0] * d[1][1] - d[0][1] * d[0][1])
    p00, p01, p11 = d[1][1] * pd, -d[0][1] * pd, d[0][0] * pd
    e00 = p00 * d[0][2] + p01 * d[1][2]
    e01 = p00 * d[0][3] + p01 * d[1][3]
    e10 = p01 * d[0][2] + p11 * d[1][2]
    e11 = p01 * d[0][3] + p11 * d[1][3]
    s00 = d[2][2] - (d[0][2] * e00 + d[1][2] * e10)
    s01 = d[2][3] - (d[0][2] * e01 + d[1][2] * e11)
    s11 = d[3][3] - (d[0][3] * e01 + d[1][3] * e11)
    sd = 1.0 / (s00 * s11 - s01 * s01)

    def apply(m):
        y0 = p00 * m[0] + p01 * m[1]
        y1 = p01 * m[0] + p11 * m[1]
        y2 = m[2] - (d[0][2] * y0 + d[1][2] * y1)
        y3 = m[3] - (d[0][3] * y0 + d[1][3] * y1)
        z2 = (s11 * y2 - s01 * y3) * sd
        z3 = (s00 * y3 - s01 * y2) * sd
        return [y0 - (e00 * z2 + e01 * z3), y1 - (e10 * z2 + e11 * z3), z2, z3]

    return apply


def product4(c, z):
    return (c[0] * z[0] + c[1] * z[1]) + (c[2] * z[2] + c[3] * z[3])


def inverse(a, left, right, jobs):
    size = a.shape[0]
    lane = lax.broadcasted_iota(jnp.int32, (8, size), 1)
    tiles = [a[8 * r : 8 * r + 8] for r in range(size // 8)]

    def rows4(tile, o):
        return [jnp.broadcast_to(tile[o + i : o + i + 1, :], (8, size)) for i in range(4)]

    def put(row, k, scaled):
        for i in range(4):
            unit = jnp.where(lane == k + i, 1.0, 0.0)
            left[k + i : k + i + 1, :] = jnp.where(lane < k, row[i], unit)[0:1]
            right[k + i : k + i + 1, :] = jnp.where(lane < k + 4, scaled[i], 0.0)[0:1]

    for t in range(size // 8):
        k = 8 * t
        columns = [
            [jnp.broadcast_to(tiles[r][:, k + j : k + j + 1], (8, size)) for j in range(8)]
            for r in range(t, size // 8)
        ]
        first = (lane >= k) & (lane < k + 4)
        second = (lane >= k + 4) & (lane < k + 8)
        row = rows4(tiles[t], 0)
        d = [rows4(column, 0) for column in columns[0]]
        d = [[d[j][i] for j in range(8)] for i in range(4)]
        apply = eliminate(d)
        scaled = apply([jnp.where(first, jnp.where(lane == k + i, 1.0, 0.0), row[i]) for i in range(4)])
        ahead = [apply([d[i][4 + j] for i in range(4)]) for j in range(4)]
        put(row, k, scaled)
        updated = []
        for r in range(t, size // 8):
            c = columns[r - t]
            tiles[r] = jnp.where(first, 0.0, tiles[r]) - product4(c, scaled)
            updated.append([c[4 + j] - product4(c, ahead[j]) for j in range(4)])
        run_next(jobs)
        row = rows4(tiles[t], 4)
        d = [rows4(column, 4) for column in updated[0]]
        d = [[d[j][i] for j in range(4)] for i in range(4)]
        apply = eliminate(d)
        scaled = apply([jnp.where(second, jnp.where(lane == k + 4 + i, 1.0, 0.0), row[i]) for i in range(4)])
        put(row, k + 4, scaled)
        for r in range(t + 1, size // 8):
            tiles[r] = jnp.where(second, 0.0, tiles[r]) - product4(updated[r - t], scaled)
        run_next(jobs)
    while jobs:
        run_next(jobs)
    return lax.dot_general(
        left[...].T,
        right[...],
        (((1,), (0,)), ((), ())),
        precision=lax.Precision.HIGHEST,
        preferred_element_type=F32,
    )


def dot(a, b):
    return lax.dot_general(a, b, (((1,), (0,)), ((), ())), preferred_element_type=F32)


def centred(values):
    return to_bf16(values - jnp.mean(values, axis=0, keepdims=True))


def stacked(values):
    hi = to_bf16(values)
    return jnp.concatenate([hi, to_bf16(values - hi.astype(F32))], axis=0)


def doubled(values):
    return jnp.concatenate([values, values], axis=1)


def eye():
    rows = lax.broadcasted_iota(jnp.int32, (LANES, LANES), 0)
    return rows == lax.broadcasted_iota(jnp.int32, (LANES, LANES), 1)


def turned(values):
    return values.T


def gram_of(spread, spread_t, variance):
    scale = spread_t.shape[0] - 1
    return dot(spread, spread_t) + jnp.where(eye(), scale * variance, 0.0)


def put_gain(gain, i, spread, values):
    gain[i] = stacked(dot(spread, values))


def change(gain, i, rows):
    return dot(rows, gain[i])


def analyse_kernel(
    order, got, other, slab_t, variance, analysed, retired, now, cent, gain, left, right, solved
):
    lags = got.shape[0]
    lag_rank, _ = ranks()
    members = slab_t.shape[0]
    block = members // lags
    mine = pl.ds(pl.multiple_of(lag_rank * block, block), block)
    own_core = lax.axis_index("core")

    def part(i):
        rows = slice(i % 2 * block, (i % 2 + 1) * block)
        values = jnp.where(own_core == i // 2, got[:, rows, :], other[:, rows, :])
        return values.reshape(members, LANES)

    chunks = [slice(LANES * c, LANES * c + LANES) for c in range(members // LANES)]
    holds = (lag_rank == order[lags - 1], lag_rank == order[lags - 2])

    def folded(values):
        return values.reshape(values.shape[0] // 8, 8, LANES).sum(axis=0)

    def centre_jobs(i, load):
        sums = []
        kept = []

        def look(rows):
            def job():
                sums.append(folded(load(rows).astype(F32)))

            return job

        def centre(rows):
            def job():
                if not kept:
                    total = sum(sums[1:], sums[0])
                    kept.append(jnp.sum(total, axis=0, keepdims=True) * (1.0 / members))
                cent[i, rows, :] = to_bf16(now[i, rows, :].astype(F32) - kept[0])

            return job

        return [look(rows) for rows in chunks] + [centre(rows) for rows in chunks]

    def gain_job(i, spread, values):
        return lambda: put_gain(gain, i, spread, values())

    spread = turned(part(0))
    gram = gram_of(spread, part(0), variance[0:1, :])

    def keep(i, load):
        def loaded(rows):
            values = load(rows)
            now[i, rows, :] = values
            return values

        return loaded

    def rows_of(i, rows):
        return got[rows.start // block : rows.stop // block, i * block : (i + 1) * block, :].reshape(LANES, LANES)

    def own_rows(rows):
        return jnp.where(holds[0], rows_of(2, rows), jnp.where(holds[1], rows_of(3, rows), slab_t[rows, :]))

    def retiring(i):
        return lambda rows: jnp.where(holds[i], slab_t[rows, :], rows_of(2 + i, rows))

    jobs = [gain_job(3, spread, lambda: part(2))]
    jobs += centre_jobs(0, keep(0, own_rows))
    jobs += [gain_job(0, spread, lambda: cent[0])]
    jobs += centre_jobs(1, keep(1, retiring(1)))
    jobs += [gain_job(1, spread, lambda: cent[1])]
    jobs += centre_jobs(2, keep(2, retiring(0)))
    jobs += [gain_job(2, spread, lambda: cent[2])]
    solved[...] = doubled(to_bf16(dot(doubled(part(1)), stacked(inverse(gram, left, right, jobs)))))
    seen = change(gain, 3, solved[...])
    spread_t = centred(part(2).astype(F32) + seen)
    innovation = to_bf16(part(3).astype(F32) - seen)
    spread = turned(spread_t)
    gram = gram_of(spread, spread_t, variance[1:2, :])

    def renewed(i):
        def load(rows):
            values = to_bf16(now[i, rows, :].astype(F32) + change(gain, i, solved[rows, :]))
            now[i, rows, :] = values
            return values

        return load

    def retire_first():
        retired[0] = to_bf16(now[2, mine, :].astype(F32) + change(gain, 2, solved[mine, :]))

    jobs = centre_jobs(0, renewed(0)) + centre_jobs(1, renewed(1)) + [retire_first]
    jobs += [gain_job(0, spread, lambda: cent[0]), gain_job(1, spread, lambda: cent[1])]
    solved_again = doubled(to_bf16(dot(doubled(innovation), stacked(inverse(gram, left, right, jobs)))))
    analysed[0] = to_bf16(now[0].astype(F32) + change(gain, 0, solved_again)).T
    solved[...] = solved_again
    retired[1] = to_bf16(now[1, mine, :].astype(F32) + change(gain, 1, solved[mine, :]))


def stay(values):
    return pltpu.with_memory_space_constraint(values, pltpu.VMEM)


def on_device(
    ensemble,
    slot_order,
    neighbour_shift,
    edge_coupling,
    observation_cells,
    observation_weight,
    observation_reading,
    observation_variance,
    observation_jitter,
):
    lags = lax.axis_size(LAG)
    spaces = lax.axis_size("zh") * lax.axis_size("core")
    per = observation_reading.shape[1]
    members = ensemble.shape[2]

    inputs = (
        ensemble,
        neighbour_shift,
        edge_coupling,
        observation_cells,
        observation_weight,
        observation_reading,
        observation_variance,
        observation_jitter,
    )
    slab_t, pieces, extra = pl.pallas_call(
        prepare_kernel,
        out_shape=[
            jax.ShapeDtypeStruct((members, LANES), BF16),
            jax.ShapeDtypeStruct((lags, FIRST_ROWS, LANES), BF16),
            jax.ShapeDtypeStruct((SECOND_ROWS - 40, LANES), BF16),
        ],
        scratch_shapes=[pltpu.VMEM((LANES, LANES), F32), pltpu.VMEM((32, LANES), F32)],
        name="prepare",
    )(*inputs)

    arrived = stay(lax.all_to_all(pieces, LAG, 0, 0, tiled=True))
    slab_t, extra = stay(slab_t), stay(extra)

    vmem = pl.BlockSpec(memory_space=pltpu.VMEM)
    smem = pl.BlockSpec(memory_space=pltpu.SMEM)
    away = pl.BlockSpec(memory_space=pl.ANY)
    sent = pl.pallas_call(
        select_kernel,
        in_specs=[smem, vmem, vmem],
        out_specs=vmem,
        out_shape=jax.ShapeDtypeStruct((spaces // 2, SECOND_ROWS, LANES), BF16),
        name="select",
    )(slot_order, arrived, extra)
    gathered = lax.all_to_all(sent, "zh", 0, 0, tiled=True)
    swapped = lax.ppermute(gathered, "core", [(0, 1), (1, 0)])
    gathered, swapped = stay(gathered), stay(swapped)

    block = members // lags
    sent = pl.pallas_call(
        observe_kernel,
        in_specs=[smem, vmem, vmem, vmem],
        out_specs=away,
        out_shape=jax.ShapeDtypeStruct((lags, THIRD * block, LANES), BF16),
        scratch_shapes=[
            pltpu.VMEM((spaces, SECOND_ROWS, LANES), BF16),
            pltpu.VMEM((spaces, 40, LANES), F32),
            pltpu.VMEM((spaces, block, LANES), BF16),
            pltpu.VMEM((2, spaces, 2 * LANES, LANES), BF16),
            pltpu.VMEM((spaces, 8, LANES), F32),
            pltpu.VMEM((3, THIRD * block, LANES), BF16),
            pltpu.SemaphoreType.DMA((lags,)),
        ],
        name="observe",
    )(slot_order, gathered, swapped, arrived)
    third = lax.all_to_all(sent, LAG, 0, 0, tiled=True)
    other = lax.ppermute(third[:, 0 : 2 * block], "core", [(0, 1), (1, 0)])
    third, other = stay(third), stay(other)

    square = pltpu.VMEM((LANES, LANES), F32)
    return pl.pallas_call(
        analyse_kernel,
        in_specs=[smem, vmem, vmem, vmem, vmem],
        out_specs=[vmem, vmem],
        out_shape=[
            jax.ShapeDtypeStruct(ensemble.shape, BF16),
            jax.ShapeDtypeStruct((CYCLES, block, LANES), BF16),
        ],
        scratch_shapes=[
            pltpu.VMEM((3, members, LANES), BF16),
            pltpu.VMEM((3, members, LANES), BF16),
            pltpu.VMEM((4, 2 * LANES, LANES), BF16),
            square,
            square,
            pltpu.VMEM((members, 2 * LANES), BF16),
        ],
        name="analyse",
    )(slot_order, third, other, slab_t, observation_variance)


def solution(mesh):
    split = Mesh(
        mesh.devices.reshape(4, 2, 4, mesh.shape["space"] // 2, 2), LAG + ("zh", "core")
    )
    space = ("zh", "core")
    placed = (
        P(LAG, space, None),
        P(),
        P(None, space),
        P(None, space),
        P(None, None, space),
        P(None, None, space),
        P(None, space),
        P(),
        P(None, space, None),
    )
    return jax.shard_map(
        on_device,
        mesh=split,
        in_specs=placed,
        out_specs=(P(LAG, space, None), P(None, LAG, space)),
        check_vma=False,
    )
```
